32 devices in a mesh: slide: 2 (over x), col: 16 (over z, y, core).
Axes of the slice: x: 2, y: 2, z: 4, core: 2. Of those that a mesh axis runs over, the one named last changes fastest.
Arguments:
- patches: bfloat16 [256, 128, 512], P(('slide', 'col')), parts along dimension 0, may hold values from -6 to 6
- tissue: int32 [256, 128], P(('slide', 'col')), parts along dimension 0, may hold values from 0 to 1, as said below
- w_query: bfloat16 [512, 512], replicated, may hold values from -0.25 to 0.25
- w_key: bfloat16 [512, 512], replicated, may hold values from -0.25 to 0.25
- w_value: bfloat16 [512, 512], replicated, may hold values from -0.25 to 0.25
- w_out: bfloat16 [512, 512], replicated, may hold values from -0.25 to 0.25
- agent_tokens: bfloat16 [256, 512], replicated, may hold values from -100 to 100
- kernel_seven: float32 [7, 7, 512], replicated, may hold values from -0.875 to 0.875
- kernel_five: float32 [5, 5, 512], replicated, may hold values from -1.25 to 1.25
- kernel_three: float32 [3, 3, 512], replicated, may hold values from -2 to 2
Outputs:
- mixed: bfloat16 [256, 128, 512], P(('slide', 'col')), parts along dimension 0
The draws below stay inside these ranges and needn't reach their ends.
There are 2 independent parts, one for each index of `slide`. The reference program is written for one: setup_inputs(seed, part) draws one part's arguments, and reference() takes and returns one part's arrays. A program takes and returns all parts, laid end to end along the dimension named above; an argument that names none is the same for every part. Nothing has to cross between parts.
Inputs may be any that keep to these rules, and one draw needn't show every extreme that they name: tissue holds 0 or 1; each slide has at least one tissue patch.
All inputs are finite; a program needn't handle non-finite values.
Results may differ from the reference program's by a relative error of at most 0.007.
The reference program's roundings to bfloat16 on the way (of `agent_values`, `token_weights` and `blended`) count: a program that leaves them out, or rounds other values in their place, can miss the bound.
Values may be sent and summed in bfloat16 or wider, within the bound.
A program may use at most 128 MiB of HBM per device.

```python
import jax
import jax.numpy as jnp
from jax import lax

D = 512
HEADS = 8
HEAD_DIM = 64
AGENTS = 256
GRID_W = 128
ROWS_DEV = 8
GRID_H = 128
N_COL = 16


def draw_tissue(key, part):
    subkeys = jax.random.split(key, 4)
    side_cells = min(GRID_H, GRID_W)
    center_rows = jax.random.randint(subkeys[0], (8,), 0, GRID_H)
    center_cols = jax.random.randint(subkeys[1], (8,), 0, GRID_W)
    radii = jax.random.randint(subkeys[2], (8,), max(side_cells // 8, 1), side_cells // 4 + 1)
    row_ids = jnp.arange(GRID_H, dtype=jnp.int32)[:, None, None]
    col_ids = jnp.arange(GRID_W, dtype=jnp.int32)[None, :, None]
    row_gap = row_ids - center_rows[None, None, :]
    col_gap = col_ids - center_cols[None, None, :]
    inside = jnp.any(row_gap * row_gap + col_gap * col_gap <= (radii * radii)[None, None, :], axis=2)
    kept_cells = jax.random.randint(subkeys[3], (GRID_H, GRID_W), 0, 8) != 0
    result = jnp.logical_and(inside, kept_cells).astype(jnp.int32)
    return result.at[center_rows[0], center_cols[0]].set(1)


def draw_agent_tokens(key, part):
    subkeys = jax.random.split(key, 1)
    return jnp.clip(3.0 * jax.random.normal(subkeys[0], (AGENTS, D), jnp.float32), -18.0, 18.0).astype(jnp.bfloat16)


def shard_levels(rng, shape, cuts, low, high):
    factor_of, own = 1.0, jax.random.fold_in(rng, 6)
    for axis_at, parts in cuts:
        heights = jnp.exp(jax.random.uniform(jax.random.fold_in(own, axis_at), (parts,), jnp.float32, low / len(cuts), high / len(cuts)))
        factor_of = factor_of * jnp.repeat(heights, shape[axis_at] // parts).reshape([-1 if axis == axis_at else 1 for axis in range(len(shape))])
    return factor_of


def bell_draw(own_key, extent, scale, reach, cuts=(), held_as=jnp.bfloat16):
    values = scale * jax.random.normal(own_key, extent, jnp.float32)
    if cuts:
        values = values * shard_levels(own_key, extent, cuts, -0.22, 0.18)
    return jnp.clip(values, -reach, reach).astype(held_as)


def setup_inputs(seed: int = 0, part: int = 0) -> dict:
    keys = jax.random.split(jax.random.key(seed), 11)
    part_splits = jax.random.split(jax.random.fold_in(keys[10], part), 11)
    return {
        "patches": bell_draw(part_splits[0], (GRID_H, GRID_W, D), 1.0, 6.0, ((0, 16),)),
        "tissue": draw_tissue(jax.random.fold_in(jax.random.fold_in(keys[10], part), 71), part),
        "w_query": bell_draw(keys[2], (D, D), D ** -0.5, 0.25),
        "w_key": bell_draw(keys[3], (D, D), D ** -0.5, 0.25),
        "w_value": bell_draw(keys[4], (D, D), D ** -0.5, 0.25),
        "w_out": bell_draw(keys[5], (D, D), D ** -0.5, 0.25),
        "agent_tokens": draw_agent_tokens(jax.random.fold_in(keys[10], 71), part),
        "kernel_seven": bell_draw(keys[7], (7, 7, D), 49 ** -0.5, 0.875, (), jnp.float32),
        "kernel_five": bell_draw(keys[8], (5, 5, D), 25 ** -0.5, 1.25, (), jnp.float32),
        "kernel_three": bell_draw(keys[9], (3, 3, D), 9 ** -0.5, 2.0, (), jnp.float32),
    }


def depthwise(extended, kernel, reach_rows, band_rows, grid_width):
    padded = jnp.pad(extended.astype(jnp.float32), ((0, 0), (reach_rows, reach_rows), (0, 0)))
    span_taps = kernel.shape[0]
    total = jnp.zeros((band_rows, grid_width, kernel.shape[2]), jnp.float32)
    for row_tap in range(span_taps):
        for col_tap in range(span_taps):
            total = total + padded[row_tap:row_tap + band_rows, col_tap:col_tap + grid_width] * kernel[row_tap, col_tap]
    return total


def reference(patches, tissue, w_query, w_key, w_value, w_out, agent_tokens, kernel_seven, kernel_five, kernel_three):
    score_scale = HEAD_DIM ** -0.5
    band_tokens = ROWS_DEV * GRID_W
    flat_tokens = patches.reshape(-1, D)
    queries = jnp.dot(flat_tokens, w_query, preferred_element_type=jnp.float32).astype(jnp.bfloat16)
    keys_all = jnp.dot(flat_tokens, w_key, preferred_element_type=jnp.float32).astype(jnp.bfloat16)
    values_all = jnp.dot(flat_tokens, w_value, preferred_element_type=jnp.float32).astype(jnp.bfloat16)
    agent_heads = agent_tokens.astype(jnp.float32).reshape(AGENTS, HEADS, HEAD_DIM)
    tissue_flat = tissue.reshape(-1)
    band_ids = jnp.arange(N_COL, dtype=jnp.int32)

    def band_stats(band_index):
        start = (band_index * band_tokens).astype(jnp.int32)
        key_band = lax.dynamic_slice_in_dim(keys_all, start, band_tokens, 0).astype(jnp.float32).reshape(band_tokens, HEADS, HEAD_DIM)
        value_band = lax.dynamic_slice_in_dim(values_all, start, band_tokens, 0).astype(jnp.float32).reshape(band_tokens, HEADS, HEAD_DIM)
        valid_band = lax.dynamic_slice_in_dim(tissue_flat, start, band_tokens, 0)[None, None, :] > 0
        scores = jnp.einsum('ahd,thd->hat', agent_heads, key_band) * score_scale
        peak_band = jnp.max(jnp.where(valid_band, scores, -1e30), axis=2)
        expo = jnp.where(valid_band, jnp.exp(scores - peak_band[:, :, None]), jnp.float32(0.0))
        total_band = jnp.sum(expo, axis=2)
        weighted_band = jnp.einsum('hat,thd->had', expo.astype(jnp.bfloat16).astype(jnp.float32), value_band)
        return peak_band, total_band, weighted_band

    band_peaks, band_totals, band_weighted = lax.map(band_stats, band_ids)
    peak = jnp.max(band_peaks, axis=0)
    factor = jnp.exp(band_peaks - peak[None])
    totals = jnp.sum(band_totals * factor, axis=0)
    weighted = jnp.sum(band_weighted * factor[..., None], axis=0)
    agent_values = (weighted / totals[..., None]).astype(jnp.bfloat16)

    value_grid = values_all.reshape(GRID_H, GRID_W, D)
    value_padded = jnp.pad(value_grid, ((3, 3), (0, 0), (0, 0)))

    def band_output(band_index):
        start = (band_index * band_tokens).astype(jnp.int32)
        query_band = lax.dynamic_slice_in_dim(queries, start, band_tokens, 0).astype(jnp.float32).reshape(band_tokens, HEADS, HEAD_DIM)
        scores = jnp.einsum('thd,ahd->tha', query_band, agent_heads) * score_scale
        top_score = jnp.max(scores, axis=2, keepdims=True)
        expo = jnp.exp(scores - top_score)
        token_weights = (expo / jnp.sum(expo, axis=2, keepdims=True)).astype(jnp.bfloat16)
        attended = jnp.einsum('tha,had->thd', token_weights.astype(jnp.float32), agent_values.astype(jnp.float32)).reshape(ROWS_DEV, GRID_W, D)
        extended = lax.dynamic_slice_in_dim(value_padded, (band_index * ROWS_DEV).astype(jnp.int32), ROWS_DEV + 6, 0)
        position = depthwise(extended, kernel_seven, 3, ROWS_DEV, GRID_W)
        position = position + depthwise(extended[1:-1], kernel_five, 2, ROWS_DEV, GRID_W)
        position = position + depthwise(extended[2:-2], kernel_three, 1, ROWS_DEV, GRID_W)
        blended = (attended + position).astype(jnp.bfloat16).reshape(band_tokens, D)
        return jnp.dot(blended, w_out, preferred_element_type=jnp.float32).astype(jnp.bfloat16).reshape(ROWS_DEV, GRID_W, D)

    return lax.map(band_output, band_ids).reshape(GRID_H, GRID_W, D)
```

```python
import functools

import jax
import jax.numpy as jnp
from jax import lax
from jax.experimental import pallas as pl
from jax.experimental.pallas import tpu as pltpu
from jax.sharding import PartitionSpec as P

HEADS = 8
LANES = 128
NONE = -1e30
F32, BF16 = jnp.float32, jnp.bfloat16
NT = (((1,), (1,)), ((), ()))
VMEM = pl.BlockSpec(memory_space=pltpu.VMEM)
LIMIT = 56 * 1024 * 1024


def low_half(shape):
    return lax.broadcasted_iota(jnp.int32, shape, len(shape) - 1) < LANES // 2


def head_agents(ag_ref, head):
    start = head // 2 * LANES
    pair = ag_ref[:, start : start + LANES].astype(F32) * 0.125
    keep = low_half(pair.shape)
    keep = keep if head % 2 == 0 else jnp.logical_not(keep)
    return jnp.where(keep, pair, 0.0).astype(BF16)


def split_agents(ag_ref, heads_ref):
    for head in range(HEADS):
        heads_ref[head, :, :] = head_agents(ag_ref, head)


def project_values(x_ref, w_ref, out_ref, ext_ref, vt_ref):
    rows, width, dim = out_ref.shape
    chunk = 256
    for c in range(0, x_ref.shape[0], chunk):
        y = jnp.dot(x_ref[c : c + chunk, :], w_ref[...], preferred_element_type=F32).astype(BF16)
        wide = y.astype(F32)
        vt_ref[:, :, c : c + chunk] = y.T.reshape(HEADS, dim // HEADS, chunk)
        for r in range(chunk // width):
            row = c // width + r
            out_ref[row, :, :] = y[r * width : (r + 1) * width, :]
            for block in range(dim // LANES):
                ext_ref[block, row + 3, 8 : width + 8, :] = wide[
                    r * width : (r + 1) * width, block * LANES : (block + 1) * LANES
                ]


def project_keys(x_ref, w_ref, out_ref):
    chunk = 256
    for c in range(0, x_ref.shape[0], chunk):
        y = jnp.dot(x_ref[c : c + chunk, :], w_ref[...], preferred_element_type=F32).astype(BF16)
        for block in range(out_ref.shape[0]):
            out_ref[block, c : c + chunk, :] = y[:, block * LANES : (block + 1) * LANES]


def token_bias(tissue_ref, bias_ref):
    rows, width = tissue_ref.shape
    for r in range(rows):
        bias = jnp.where(tissue_ref[r : r + 1, :] > 0, 0.0, NONE)
        bias_ref[r * width : (r + 1) * width, :] = jnp.broadcast_to(bias, (LANES, width)).T


def band_stats(pair, bias_ref, heads_ref, k_ref, vt_ref, score_ref, w_ref, mt_ref):
    tokens = k_ref.shape[1]
    agents = heads_ref.shape[1]
    chunk = 256
    tops = []
    for side in range(2):
        top = jnp.full((8, agents), NONE, F32)
        for c in range(0, tokens, chunk):
            s = lax.dot_general(
                k_ref[pair, c : c + chunk, :], heads_ref[2 * pair + side], NT, preferred_element_type=F32
            )
            bias = bias_ref[c : c + chunk, :]
            s = s + jnp.concatenate([bias] * (agents // LANES), axis=1)
            score_ref[side, c : c + chunk, :] = s
            top = jnp.maximum(top, jnp.max(s.reshape(chunk // 8, 8, agents), axis=0))
        tops.append(jnp.max(top, axis=0, keepdims=True))
    for side in range(2):
        head = 2 * pair + side
        top = jnp.maximum(tops[side], 0.1 * NONE)
        total = jnp.zeros((8, agents), F32)
        got = None
        for c in range(0, tokens, chunk):
            e = jnp.exp(score_ref[side, c : c + chunk, :] - top)
            total = total + jnp.sum(e.reshape(chunk // 8, 8, agents), axis=0)
            part = jnp.dot(vt_ref[head, :, c : c + chunk], e.astype(BF16), preferred_element_type=F32)
            got = part if got is None else got + part
        w_ref[head, :, :] = got
        mt_ref[head, 0:1, :] = tops[side]
        mt_ref[head, 1:2, :] = jnp.sum(total, axis=0, keepdims=True)


def token_side(x_ref, wq_ref, heads_ref, tw_ref):
    tokens = x_ref.shape[0]
    chunk = 256
    for c in range(0, tokens, chunk):
        q = jnp.dot(x_ref[c : c + chunk, :], wq_ref[...], preferred_element_type=F32).astype(BF16)
        for head in range(HEADS):
            start = head // 2 * LANES
            s = lax.dot_general(
                heads_ref[head], q[:, start : start + LANES], NT, preferred_element_type=F32
            )
            e = jnp.exp(s - jnp.max(s, axis=0, keepdims=True))
            share = 1.0 / jnp.sum(e, axis=0, keepdims=True)
            tw_ref[head, :, c : c + chunk] = (e * share).astype(BF16)


def spread_taps(k7_ref, k5_ref, k3_ref, taps_ref):
    for block in range(taps_ref.shape[0]):
        at = slice(block * LANES, block * LANES + LANES)
        for p in range(7):
            for q in range(7):
                tap = k7_ref[p, q : q + 1, at]
                if 1 <= p <= 5 and 1 <= q <= 5:
                    tap = tap + k5_ref[p - 1, q - 1 : q, at]
                if 2 <= p <= 4 and 2 <= q <= 4:
                    tap = tap + k3_ref[p - 2, q - 2 : q - 1, at]
                taps_ref[block, p * 7 + q, :, :] = jnp.broadcast_to(tap, (8, LANES))


def fill_sides(ext_ref):
    blocks, ext_rows, padded, _ = ext_ref.shape
    for block in range(blocks):
        for r in range(ext_rows):
            ext_ref[block, r, 0:8, :] = jnp.zeros((8, LANES), F32)
            ext_ref[block, r, padded - 8 : padded, :] = jnp.zeros((8, LANES), F32)


def fill_rim(rim_ref, ext_ref, first):
    width = rim_ref.shape[1]
    for block in range(ext_ref.shape[0]):
        at = slice(block * LANES, block * LANES + LANES)
        for r in range(3):
            ext_ref[block, first + r, 8 : width + 8, :] = rim_ref[r, :, at].astype(F32)


def convolve(ext_ref, taps_ref, pos_ref, part, parts):
    blocks, ext_rows, _, _ = ext_ref.shape
    _, rows, width, _ = pos_ref.shape
    step = 8

    def one(block, carry):
        for c in range(0, width, step):
            sums = [None] * rows
            for q in range(7):
                taps = [taps_ref[block, p * 7 + q] for p in range(7)]
                for r in range(ext_rows):
                    x = ext_ref[block, r, c + 5 + q : c + 5 + q + step, :]
                    for out in range(max(r - 6, 0), min(r + 1, rows)):
                        term = x * taps[r - out]
                        sums[out] = term if sums[out] is None else sums[out] + term
            for out in range(rows):
                pos_ref[block, out, c : c + step, :] = sums[out]
        return carry

    lax.fori_loop(part * blocks // parts, (part + 1) * blocks // parts, one, 0)


def blend(av_t, tw_ref, pos_ref, out_ref):
    blocks, _, width, _ = pos_ref.shape
    chunk = 256
    for c in range(0, out_ref.shape[0], chunk):
        parts = []
        for head in range(HEADS):
            parts.append(
                jnp.dot(
                    av_t[head * 64 : head * 64 + 64, :],
                    tw_ref[head, :, c : c + chunk],
                    preferred_element_type=F32,
                )
            )
        attended = jnp.concatenate(parts, axis=0).T
        position = jnp.concatenate(
            [
                jnp.concatenate([pos_ref[b, r] for b in range(blocks)], axis=1)
                for r in range(c // width, (c + chunk) // width)
            ],
            axis=0,
        )
        out_ref[c : c + chunk, :] = (attended + position).astype(BF16)


class Exchange:
    def __init__(self, n, v_ref, refs, sems):
        self.n, self.me = n, lax.axis_index("col")
        (self.w, self.mt, self.wp, self.mtp, self.ws, self.ms, self.wr, self.mr, self.av,
         above_ref, below_ref) = refs
        s1, r1, s2, r2, s3, r3, s4, r4 = sems
        me, m = self.me, n // 2
        self.m = m
        self.low, self.group = lax.rem(me, 2), me // 2
        twin = me + 1 - 2 * self.low
        self.to = [lax.rem(me + k, n) for k in range(1, n)]
        rows = v_ref.shape[0]
        half = HEADS // 2
        self.mine, self.other = half * self.low, half * (1 - self.low)

        def remote(src, dst, s, r, peer):
            return pltpu.make_async_remote_copy(
                src_ref=src, dst_ref=dst, send_sem=s, recv_sem=r,
                device_id={"col": peer}, device_id_type=pl.DeviceIdType.MESH,
            )

        self.swap = [
            remote(self.w.at[pl.ds(self.other, half)], self.wp, s1.at[0], r1.at[0], twin),
            remote(self.mt.at[pl.ds(self.other, half)], self.mtp, s1.at[1], r1.at[1], twin),
        ]
        self.scatter = []
        for k in range(1, m):
            g = lax.rem(self.group + k, m)
            peer = 2 * g + self.low
            self.scatter.append(
                remote(self.ws.at[g], self.wr.at[self.group], s2.at[0, k - 1], r2.at[0, k - 1], peer)
            )
            self.scatter.append(
                remote(self.ms.at[g], self.mr.at[self.group], s2.at[1, k - 1], r2.at[1, k - 1], peer)
            )
        self.slot = m * self.low + self.group
        self.gather = [
            remote(self.av.at[self.slot], self.av.at[self.slot], s4.at[k], r4.at[k], p)
            for k, p in enumerate(self.to)
        ]
        self.down = remote(v_ref.at[pl.ds(rows - 3, 3)], above_ref, s3.at[0], r3.at[0], lax.rem(me + 1, n))
        self.up = remote(v_ref.at[pl.ds(0, 3)], below_ref, s3.at[1], r3.at[1], lax.rem(me + n - 1, n))

    def greet(self):
        barrier = pltpu.get_barrier_semaphore()
        for p in self.to:
            pl.semaphore_signal(
                barrier, inc=1, device_id={"col": p}, device_id_type=pl.DeviceIdType.MESH
            )

    def met(self):
        pl.semaphore_wait(pltpu.get_barrier_semaphore(), self.n - 1)

    def send_rims(self):
        @pl.when(self.me < self.n - 1)
        def _():
            self.down.start()

        @pl.when(self.me > 0)
        def _():
            self.up.start()

    def send_twin(self):
        for copy in self.swap:
            copy.start()

    def merge(self):
        for copy in self.swap:
            copy.wait()
        half, depth, _ = self.wp.shape
        piece = self.ws.shape[1]
        for h in range(half):
            a, b = self.mt[self.mine + h], self.mtp[h]
            top = jnp.maximum(a[0:1], b[0:1])
            fa, fb = jnp.exp(a[0:1] - top), jnp.exp(b[0:1] - top)
            total = a[1:2] * fa + b[1:2] * fb
            w = self.w[self.mine + h] * fa + self.wp[h] * fb
            for p in range(depth // piece):
                at = h * depth // piece + p
                self.ws[at] = w[p * piece : (p + 1) * piece]
                self.ms[at, 0:1, :] = top
                self.ms[at, 1:2, :] = total
        for copy in self.scatter:
            copy.start()
        self.wr[self.group] = self.ws[self.group]
        self.mr[self.group] = self.ms[self.group]

    def reduce(self):
        for copy in self.scatter:
            copy.wait()
        tops = [self.mr[i, 0:1, :] for i in range(self.m)]
        top = functools.reduce(jnp.maximum, tops)
        total, weighted = 0.0, 0.0
        for i in range(self.m):
            f = jnp.exp(tops[i] - top)
            total = total + f * self.mr[i, 1:2, :]
            weighted = weighted + f * self.wr[i]
        self.av[self.slot] = (weighted / total).astype(BF16)
        for copy in self.gather:
            copy.start()

    def rims(self):
        @pl.when(self.me < self.n - 1)
        def _():
            self.down.wait_send()
            self.up.wait_recv()

        @pl.when(self.me > 0)
        def _():
            self.down.wait_recv()
            self.up.wait_send()

    def end(self):
        for copy in self.gather:
            copy.wait()


def sem_shapes(n):
    dma = pltpu.SemaphoreType.DMA
    m = n // 2
    return [dma((2,)), dma((2,)), dma((2, m - 1)), dma((2, m - 1)), dma((2,)), dma((2,)),
            dma((n - 1,)), dma((n - 1,))]


def whole_kernel(n, *refs):
    sources, out_ref = refs[:9], refs[9]
    held, load_sem = refs[10:19], refs[19]
    x_ref, tissue_ref, wq_ref, wk_ref, wv_ref, ag_ref, k7_ref, k5_ref, k3_ref = held
    (v_ref, vt_ref, k_ref, bias_ref, score_ref, tw_ref, taps_ref, ext_ref, pos_ref, heads_ref) = refs[20:30]
    shared, sems = refs[30:41], refs[41:]
    w_ref, mt_ref, av_ref, above_ref, below_ref = shared[0], shared[1], shared[8], shared[9], shared[10]
    loads = [pltpu.make_async_copy(sources[i], held[i], load_sem.at[i]) for i in range(9)]
    for i in (0, 4, 3, 5, 1, 6, 7, 8, 2):
        loads[i].start()
    work = Exchange(n, v_ref, shared, sems)
    above_ref[...] = jnp.zeros(above_ref.shape, BF16)
    below_ref[...] = jnp.zeros(below_ref.shape, BF16)
    work.greet()
    fill_sides(ext_ref)
    loads[0].wait()
    loads[4].wait()
    project_values(x_ref, wv_ref, v_ref, ext_ref, vt_ref)
    work.met()
    work.send_rims()
    loads[5].wait()
    split_agents(ag_ref, heads_ref)
    loads[1].wait()
    token_bias(tissue_ref, bias_ref)
    loads[3].wait()
    project_keys(x_ref, wk_ref, k_ref)

    def stats(pair, carry):
        band_stats(pair, bias_ref, heads_ref, k_ref, vt_ref, score_ref, w_ref, mt_ref)
        return carry

    lax.fori_loop(work.other // 2, work.other // 2 + HEADS // 4, stats, 0)
    work.send_twin()
    lax.fori_loop(work.mine // 2, work.mine // 2 + HEADS // 4, stats, 0)
    work.merge()
    for i in (6, 7, 8, 2):
        loads[i].wait()
    spread_taps(k7_ref, k5_ref, k3_ref, taps_ref)
    token_side(x_ref, wq_ref, heads_ref, tw_ref)
    work.rims()
    fill_rim(above_ref, ext_ref, 0)
    fill_rim(below_ref, ext_ref, ext_ref.shape[1] - 3)
    convolve(ext_ref, taps_ref, pos_ref, 0, 2)
    work.reduce()
    convolve(ext_ref, taps_ref, pos_ref, 1, 2)
    work.end()
    av_t = jnp.concatenate([av_ref[i] for i in range(n)], axis=0)
    blend(av_t, tw_ref, pos_ref, out_ref)


def on_device(n, patches, tissue, w_query, w_key, w_value, w_out, agent_tokens, k7, k5, k3):
    rows, width, dim = patches.shape
    tokens = rows * width
    agents = agent_tokens.shape[0]
    x = patches.reshape(tokens, dim)
    rim = (3, width, dim)
    blocks = dim // LANES
    depth, half, m = dim // HEADS, HEADS // 2, n // 2
    piece = dim // n
    given = (x, tissue, w_query, w_key, w_value, agent_tokens, k7, k5, k3)
    blended = pl.pallas_call(
        functools.partial(whole_kernel, n),
        out_shape=jax.ShapeDtypeStruct((tokens, dim), BF16),
        in_specs=[pl.BlockSpec(memory_space=pltpu.HBM)] * len(given),
        out_specs=VMEM,
        scratch_shapes=[pltpu.VMEM(a.shape, a.dtype) for a in given]
        + [
            pltpu.SemaphoreType.DMA((len(given),)),
            pltpu.VMEM((rows, width, dim), BF16),
            pltpu.VMEM((HEADS, depth, tokens), BF16),
            pltpu.VMEM((blocks, tokens, LANES), BF16),
            pltpu.VMEM((tokens, LANES), F32),
            pltpu.VMEM((2, tokens, agents), F32),
            pltpu.VMEM((HEADS, agents, tokens), BF16),
            pltpu.VMEM((blocks, 49, 8, LANES), F32),
            pltpu.VMEM((blocks, rows + 6, width + 16, LANES), F32),
            pltpu.VMEM((blocks, rows, width, LANES), F32),
            pltpu.VMEM((HEADS, agents, LANES), BF16),
            pltpu.VMEM((HEADS, depth, agents), F32),
            pltpu.VMEM((HEADS, 2, agents), F32),
            pltpu.VMEM((half, depth, agents), F32),
            pltpu.VMEM((half, 2, agents), F32),
            pltpu.VMEM((m, piece, agents), F32),
            pltpu.VMEM((m, 2, agents), F32),
            pltpu.VMEM((m, piece, agents), F32),
            pltpu.VMEM((m, 2, agents), F32),
            pltpu.VMEM((n, piece, agents), BF16),
            pltpu.VMEM(rim, BF16),
            pltpu.VMEM(rim, BF16),
        ]
        + sem_shapes(n),
        compiler_params=pltpu.CompilerParams(
            vmem_limit_bytes=LIMIT, collective_id=0, has_side_effects=True
        ),
    )(*given)
    mixed = jnp.dot(blended, w_out, preferred_element_type=F32).astype(BF16)
    return mixed.reshape(rows, width, dim)


def solution(mesh):
    rows = P(("slide", "col"), None, None)
    return jax.shard_map(
        functools.partial(on_device, mesh.shape["col"]),
        mesh=mesh,
        in_specs=(rows, P(("slide", "col"), None)) + (P(),) * 8,
        out_specs=rows,
        check_vma=False,
    )
```

```python
import functools

import jax
import jax.numpy as jnp
from jax import lax
from jax.experimental import pallas as pl
from jax.experimental.pallas import tpu as pltpu
from jax.sharding import PartitionSpec as P

HEADS = 8
LANES = 128
NONE = -1e30
F32, BF16 = jnp.float32, jnp.bfloat16
NT = (((1,), (1,)), ((), ()))
VMEM = pl.BlockSpec(memory_space=pltpu.VMEM)
LIMIT = 56 * 1024 * 1024


def low_half(shape):
    return lax.broadcasted_iota(jnp.int32, shape, len(shape) - 1) < LANES // 2


def head_agents(ag_ref, head):
    start = head // 2 * LANES
    pair = ag_ref[:, start : start + LANES].astype(F32) * 0.125
    keep = low_half(pair.shape)
    keep = keep if head % 2 == 0 else jnp.logical_not(keep)
    return jnp.where(keep, pair, 0.0).astype(BF16)


def split_agents(ag_ref, heads_ref):
    for head in range(HEADS):
        heads_ref[head, :, :] = head_agents(ag_ref, head)


def project_values(x_ref, w_ref, out_ref, vt_ref):
    rows, width, dim = out_ref.shape
    chunk = 256
    for c in range(0, x_ref.shape[0], chunk):
        y = jnp.dot(x_ref[c : c + chunk, :], w_ref[...], preferred_element_type=F32).astype(BF16)
        vt_ref[:, :, c : c + chunk] = y.T.reshape(HEADS, dim // HEADS, chunk)
        for r in range(chunk // width):
            out_ref[c // width + r, :, :] = y[r * width : (r + 1) * width, :]


def project_keys(x_ref, w_ref, out_ref):
    chunk = 256
    for c in range(0, x_ref.shape[0], chunk):
        y = jnp.dot(x_ref[c : c + chunk, :], w_ref[...], preferred_element_type=F32).astype(BF16)
        for block in range(out_ref.shape[0]):
            out_ref[block, c : c + chunk, :] = y[:, block * LANES : (block + 1) * LANES]


def token_bias(tissue_ref, bias_ref):
    rows, width = tissue_ref.shape
    for r in range(rows):
        bias = jnp.where(tissue_ref[r : r + 1, :] > 0, 0.0, NONE)
        bias_ref[r * width : (r + 1) * width, :] = jnp.broadcast_to(bias, (LANES, width)).T


def band_stats(pair, bias_ref, heads_ref, k_ref, vt_ref, score_ref, w_ref, mt_ref):
    tokens = k_ref.shape[1]
    agents = heads_ref.shape[1]
    chunk = 256
    tops = []
    for side in range(2):
        top = jnp.full((8, agents), NONE, F32)
        for c in range(0, tokens, chunk):
            s = lax.dot_general(
                k_ref[pair, c : c + chunk, :], heads_ref[2 * pair + side], NT, preferred_element_type=F32
            )
            bias = bias_ref[c : c + chunk, :]
            s = s + jnp.concatenate([bias] * (agents // LANES), axis=1)
            score_ref[side, c : c + chunk, :] = s
            top = jnp.maximum(top, jnp.max(s.reshape(chunk // 8, 8, agents), axis=0))
        tops.append(jnp.max(top, axis=0, keepdims=True))
    for side in range(2):
        head = 2 * pair + side
        top = jnp.maximum(tops[side], 0.1 * NONE)
        total = jnp.zeros((8, agents), F32)
        got = None
        for c in range(0, tokens, chunk):
            e = jnp.exp(score_ref[side, c : c + chunk, :] - top)
            total = total + jnp.sum(e.reshape(chunk // 8, 8, agents), axis=0)
            part = jnp.dot(vt_ref[head, :, c : c + chunk], e.astype(BF16), preferred_element_type=F32)
            got = part if got is None else got + part
        w_ref[head, :, :] = got
        mt_ref[head, 0:1, :] = tops[side]
        mt_ref[head, 1:2, :] = jnp.sum(total, axis=0, keepdims=True)


def token_side(x_ref, wq_ref, heads_ref, tw_ref):
    tokens = x_ref.shape[0]
    chunk = 256
    for c in range(0, tokens, chunk):
        q = jnp.dot(x_ref[c : c + chunk, :], wq_ref[...], preferred_element_type=F32).astype(BF16)
        for head in range(HEADS):
            start = head // 2 * LANES
            s = lax.dot_general(
                heads_ref[head], q[:, start : start + LANES], NT, preferred_element_type=F32
            )
            e = jnp.exp(s - jnp.max(s, axis=0, keepdims=True))
            share = 1.0 / jnp.sum(e, axis=0, keepdims=True)
            tw_ref[head, :, c : c + chunk] = (e * share).astype(BF16)


POINTS = (1.0, -1.0, 2.0, -2.0, 0.5, -0.5)
NORMS = (-4.5, 4.5, 45.0, -45.0, 2.8125, -2.8125)
PLANES = 13


def spread_taps(k7_ref, k5_ref, k3_ref, sum_ref, taps_ref):
    for p in range(7):
        sum_ref[p, 0:7, :] = k7_ref[p]
    for p in range(5):
        sum_ref[p + 1, 1:6, :] = sum_ref[p + 1, 1:6, :] + k5_ref[p]
    for p in range(3):
        sum_ref[p + 2, 2:5, :] = sum_ref[p + 2, 2:5, :] + k3_ref[p]

    def one(block, carry):
        at = pl.ds(pl.multiple_of(block * LANES, LANES), LANES)
        g = [sum_ref[p, 0:7, at] for p in range(7)]
        planes = []
        for first, count in ((0, 4), (4, 3)):
            for point, norm in zip(POINTS, NORMS):
                total = g[first] * (1.0 / norm)
                for j in range(1, count):
                    total = total + g[first + j] * (point**j / norm)
                planes.append(total)
        planes.append(g[3])
        for i, plane in enumerate(planes):
            for q in range(7):
                taps_ref[block, i * 7 + q, :, :] = jnp.broadcast_to(plane[q : q + 1], (8, LANES))
        return carry

    lax.fori_loop(0, taps_ref.shape[0], one, 0)


def fill_sides(ext_ref):
    blocks, planes, padded, _ = ext_ref.shape
    for block in range(blocks):
        for r in range(planes):
            ext_ref[block, r, 0:8, :] = jnp.zeros((8, LANES), F32)
            ext_ref[block, r, padded - 8 : padded, :] = jnp.zeros((8, LANES), F32)


def at_points(d, last):
    planes = []
    e, o = d[0] + d[4] - 4.25 * d[2], d[1] + d[5] - 4.25 * d[3]
    planes += [o + e, o - e]
    e, o = 0.5 * d[0] - 2.5 * d[2] + 2.0 * d[4], 0.25 * d[1] - 1.25 * d[3] + d[5]
    planes += [o + e, o - e]
    e, o = 2.0 * d[0] - 2.5 * d[2] + 0.5 * d[4], 4.0 * d[1] - 5.0 * d[3] + d[5]
    planes += [o + e, o - e]
    if last:
        planes.append(d[6] - d[0] + 5.25 * (d[2] - d[4]))
    return planes


def transform(v_ref, above_ref, below_ref, ext_ref):
    blocks = ext_ref.shape[0]
    rows, width, _ = v_ref.shape
    step = 16

    def one(block, carry):
        at = pl.ds(pl.multiple_of(block * LANES, LANES), LANES)
        for c in range(0, width, step):
            where = slice(c, c + step)
            d = [above_ref[r, where, at].astype(F32) for r in range(3)]
            d += [v_ref[r, where, at].astype(F32) for r in range(rows)]
            d += [below_ref[r, where, at].astype(F32) for r in range(3)]
            planes = at_points(d[0:7], True) + at_points(d[4:11], True) + at_points(d[8:14], False)
            for i, plane in enumerate(planes):
                ext_ref[block, i, c + 8 : c + 8 + step, :] = plane
        return carry

    lax.fori_loop(0, blocks, one, 0)


def convolve(ext_ref, taps_ref, pos_ref, part, parts):
    blocks = ext_ref.shape[0]
    width = pos_ref.shape[2]
    step = 16

    def one(block, carry):
        for c in range(0, width, step):
            sums = [[None] * 7, [None] * 7]
            for q in range(7):
                x = [ext_ref[block, i, c + 5 + q : c + 5 + q + step, :] for i in range(20)]
                for k in range(PLANES):
                    tap = taps_ref[block, k * 7 + q]
                    tap = jnp.concatenate([tap] * (step // 8), axis=0)
                    point, first = (6, 0) if k == 12 else (k % 6, k // 6)
                    for tile in range(2):
                        term = x[(first + tile) * 7 + point] * tap
                        old = sums[tile][point]
                        sums[tile][point] = term if old is None else old + term
            for tile in range(2):
                m = sums[tile]
                s1, d1 = m[0] + m[1], m[0] - m[1]
                s2, d2 = m[2] + m[3], m[2] - m[3]
                s3, d3 = m[4] + m[5], m[4] - m[5]
                outs = (
                    s1 + s2 + s3,
                    d1 + 2.0 * d2 + 0.5 * d3,
                    s1 + 4.0 * s2 + 0.25 * s3,
                    d1 + 8.0 * d2 + 0.125 * d3 + m[6],
                )
                for i, y in enumerate(outs):
                    pos_ref[block, tile * 4 + i, c : c + step, :] = y
        return carry

    lax.fori_loop(part * blocks // parts, (part + 1) * blocks // parts, one, 0)


def blend(av_t, tw_ref, pos_ref, out_ref):
    blocks, _, width, _ = pos_ref.shape
    chunk = 256
    for c in range(0, out_ref.shape[0], chunk):
        parts = []
        for head in range(HEADS):
            parts.append(
                jnp.dot(
                    av_t[head * 64 : head * 64 + 64, :],
                    tw_ref[head, :, c : c + chunk],
                    preferred_element_type=F32,
                )
            )
        attended = jnp.concatenate(parts, axis=0).T
        position = jnp.concatenate(
            [
                jnp.concatenate([pos_ref[b, r] for b in range(blocks)], axis=1)
                for r in range(c // width, (c + chunk) // width)
            ],
            axis=0,
        )
        out_ref[c : c + chunk, :] = (attended + position).astype(BF16)


class Exchange:
    def __init__(self, n, v_ref, refs, sems):
        self.n, self.me = n, lax.axis_index("col")
        (self.w, self.mt, self.wp, self.mtp, self.ws, self.ms, self.wr, self.mr, self.av,
         above_ref, below_ref) = refs
        s1, r1, s2, r2, s3, r3, s4, r4 = sems
        me, m = self.me, n // 2
        self.m = m
        self.low, self.group = lax.rem(me, 2), me // 2
        twin = me + 1 - 2 * self.low
        self.to = [lax.rem(me + k, n) for k in range(1, n)]
        rows = v_ref.shape[0]
        half = HEADS // 2
        self.mine, self.other = half * self.low, half * (1 - self.low)

        def remote(src, dst, s, r, peer):
            return pltpu.make_async_remote_copy(
                src_ref=src, dst_ref=dst, send_sem=s, recv_sem=r,
                device_id={"col": peer}, device_id_type=pl.DeviceIdType.MESH,
            )

        self.swap = [
            remote(self.w.at[pl.ds(self.other, half)], self.wp, s1.at[0], r1.at[0], twin),
            remote(self.mt.at[pl.ds(self.other, half)], self.mtp, s1.at[1], r1.at[1], twin),
        ]
        self.scatter = []
        for k in range(1, m):
            g = lax.rem(self.group + k, m)
            peer = 2 * g + self.low
            self.scatter.append(
                remote(self.ws.at[g], self.wr.at[self.group], s2.at[0, k - 1], r2.at[0, k - 1], peer)
            )
            self.scatter.append(
                remote(self.ms.at[g], self.mr.at[self.group], s2.at[1, k - 1], r2.at[1, k - 1], peer)
            )
        self.slot = m * self.low + self.group
        self.gather = [
            remote(self.av.at[self.slot], self.av.at[self.slot], s4.at[k], r4.at[k], p)
            for k, p in enumerate(self.to)
        ]
        self.down = remote(v_ref.at[pl.ds(rows - 3, 3)], above_ref, s3.at[0], r3.at[0], lax.rem(me + 1, n))
        self.up = remote(v_ref.at[pl.ds(0, 3)], below_ref, s3.at[1], r3.at[1], lax.rem(me + n - 1, n))

    def greet(self):
        barrier = pltpu.get_barrier_semaphore()
        for p in self.to:
            pl.semaphore_signal(
                barrier, inc=1, device_id={"col": p}, device_id_type=pl.DeviceIdType.MESH
            )

    def met(self):
        pl.semaphore_wait(pltpu.get_barrier_semaphore(), self.n - 1)

    def send_rims(self):
        @pl.when(self.me < self.n - 1)
        def _():
            self.down.start()

        @pl.when(self.me > 0)
        def _():
            self.up.start()

    def send_twin(self):
        for copy in self.swap:
            copy.start()

    def merge(self):
        for copy in self.swap:
            copy.wait()
        half, depth, _ = self.wp.shape
        piece = self.ws.shape[1]
        for h in range(half):
            a, b = self.mt[self.mine + h], self.mtp[h]
            top = jnp.maximum(a[0:1], b[0:1])
            fa, fb = jnp.exp(a[0:1] - top), jnp.exp(b[0:1] - top)
            total = a[1:2] * fa + b[1:2] * fb
            w = self.w[self.mine + h] * fa + self.wp[h] * fb
            for p in range(depth // piece):
                at = h * depth // piece + p
                self.ws[at] = w[p * piece : (p + 1) * piece]
                self.ms[at, 0:1, :] = top
                self.ms[at, 1:2, :] = total
        for copy in self.scatter:
            copy.start()
        self.wr[self.group] = self.ws[self.group]
        self.mr[self.group] = self.ms[self.group]

    def reduce(self):
        for copy in self.scatter:
            copy.wait()
        tops = [self.mr[i, 0:1, :] for i in range(self.m)]
        top = functools.reduce(jnp.maximum, tops)
        total, weighted = 0.0, 0.0
        for i in range(self.m):
            f = jnp.exp(tops[i] - top)
            total = total + f * self.mr[i, 1:2, :]
            weighted = weighted + f * self.wr[i]
        self.av[self.slot] = (weighted / total).astype(BF16)
        for copy in self.gather:
            copy.start()

    def rims(self):
        @pl.when(self.me < self.n - 1)
        def _():
            self.down.wait_send()
            self.up.wait_recv()

        @pl.when(self.me > 0)
        def _():
            self.down.wait_recv()
            self.up.wait_send()

    def end(self):
        for copy in self.gather:
            copy.wait()


def sem_shapes(n):
    dma = pltpu.SemaphoreType.DMA
    m = n // 2
    return [dma((2,)), dma((2,)), dma((2, m - 1)), dma((2, m - 1)), dma((2,)), dma((2,)),
            dma((n - 1,)), dma((n - 1,))]


def whole_kernel(n, *refs):
    sources, out_ref = refs[:9], refs[9]
    held, load_sem = refs[10:19], refs[19]
    x_ref, tissue_ref, wq_ref, wk_ref, wv_ref, ag_ref, k7_ref, k5_ref, k3_ref = held
    (v_ref, vt_ref, k_ref, bias_ref, score_ref, tw_ref, sum_ref, taps_ref, ext_ref, pos_ref, heads_ref) = refs[20:31]
    shared, sems = refs[31:42], refs[42:]
    w_ref, mt_ref, av_ref, above_ref, below_ref = shared[0], shared[1], shared[8], shared[9], shared[10]
    loads = [pltpu.make_async_copy(sources[i], held[i], load_sem.at[i]) for i in range(9)]
    for i in (0, 4, 3, 5, 1, 6, 7, 8, 2):
        loads[i].start()
    work = Exchange(n, v_ref, shared, sems)
    above_ref[...] = jnp.zeros(above_ref.shape, BF16)
    below_ref[...] = jnp.zeros(below_ref.shape, BF16)
    work.greet()
    fill_sides(ext_ref)
    loads[0].wait()
    loads[4].wait()
    project_values(x_ref, wv_ref, v_ref, vt_ref)
    work.met()
    work.send_rims()
    loads[5].wait()
    split_agents(ag_ref, heads_ref)
    loads[1].wait()
    token_bias(tissue_ref, bias_ref)
    loads[3].wait()
    project_keys(x_ref, wk_ref, k_ref)

    def stats(pair, carry):
        band_stats(pair, bias_ref, heads_ref, k_ref, vt_ref, score_ref, w_ref, mt_ref)
        return carry

    lax.fori_loop(work.other // 2, work.other // 2 + HEADS // 4, stats, 0)
    work.send_twin()
    lax.fori_loop(work.mine // 2, work.mine // 2 + HEADS // 4, stats, 0)
    work.merge()
    for i in (6, 7, 8, 2):
        loads[i].wait()
    spread_taps(k7_ref, k5_ref, k3_ref, sum_ref, taps_ref)
    token_side(x_ref, wq_ref, heads_ref, tw_ref)
    work.rims()
    transform(v_ref, above_ref, below_ref, ext_ref)
    convolve(ext_ref, taps_ref, pos_ref, 0, 2)
    work.reduce()
    convolve(ext_ref, taps_ref, pos_ref, 1, 2)
    work.end()
    av_t = jnp.concatenate([av_ref[i] for i in range(n)], axis=0)
    blend(av_t, tw_ref, pos_ref, out_ref)


def on_device(n, patches, tissue, w_query, w_key, w_value, w_out, agent_tokens, k7, k5, k3):
    rows, width, dim = patches.shape
    tokens = rows * width
    agents = agent_tokens.shape[0]
    x = patches.reshape(tokens, dim)
    rim = (3, width, dim)
    blocks = dim // LANES
    depth, half, m = dim // HEADS, HEADS // 2, n // 2
    piece = dim // n
    given = (x, tissue, w_query, w_key, w_value, agent_tokens, k7, k5, k3)
    blended = pl.pallas_call(
        functools.partial(whole_kernel, n),
        out_shape=jax.ShapeDtypeStruct((tokens, dim), BF16),
        in_specs=[pl.BlockSpec(memory_space=pltpu.HBM)] * len(given),
        out_specs=VMEM,
        scratch_shapes=[pltpu.VMEM(a.shape, a.dtype) for a in given]
        + [
            pltpu.SemaphoreType.DMA((len(given),)),
            pltpu.VMEM((rows, width, dim), BF16),
            pltpu.VMEM((HEADS, depth, tokens), BF16),
            pltpu.VMEM((blocks, tokens, LANES), BF16),
            pltpu.VMEM((tokens, LANES), F32),
            pltpu.VMEM((2, tokens, agents), F32),
            pltpu.VMEM((HEADS, agents, tokens), BF16),
            pltpu.VMEM((7, 8, dim), F32),
            pltpu.VMEM((blocks, 7 * PLANES, 8, LANES), F32),
            pltpu.VMEM((blocks, 20, width + 16, LANES), F32),
            pltpu.VMEM((blocks, rows, width, LANES), F32),
            pltpu.VMEM((HEADS, agents, LANES), BF16),
            pltpu.VMEM((HEADS, depth, agents), F32),
            pltpu.VMEM((HEADS, 2, agents), F32),
            pltpu.VMEM((half, depth, agents), F32),
            pltpu.VMEM((half, 2, agents), F32),
            pltpu.VMEM((m, piece, agents), F32),
            pltpu.VMEM((m, 2, agents), F32),
            pltpu.VMEM((m, piece, agents), F32),
            pltpu.VMEM((m, 2, agents), F32),
            pltpu.VMEM((n, piece, agents), BF16),
            pltpu.VMEM(rim, BF16),
            pltpu.VMEM(rim, BF16),
        ]
        + sem_shapes(n),
        compiler_params=pltpu.CompilerParams(
            vmem_limit_bytes=LIMIT, collective_id=0, has_side_effects=True
        ),
    )(*given)
    mixed = jnp.dot(blended, w_out, preferred_element_type=F32).astype(BF16)
    return mixed.reshape(rows, width, dim)


def solution(mesh):
    rows = P(("slide", "col"), None, None)
    return jax.shard_map(
        functools.partial(on_device, mesh.shape["col"]),
        mesh=mesh,
        in_specs=(rows, P(("slide", "col"), None)) + (P(),) * 8,
        out_specs=rows,
        check_vma=False,
    )
```

```python
import functools

import jax
import jax.numpy as jnp
from jax import lax
from jax.experimental import pallas as pl
from jax.experimental.pallas import tpu as pltpu
from jax.sharding import PartitionSpec as P

HEADS = 8
LANES = 128
NONE = -1e30
F32, BF16 = jnp.float32, jnp.bfloat16
NT = (((1,), (1,)), ((), ()))
VMEM = pl.BlockSpec(memory_space=pltpu.VMEM)
LIMIT = 56 * 1024 * 1024


def low_half(shape):
    return lax.broadcasted_iota(jnp.int32, shape, len(shape) - 1) < LANES // 2


def head_agents(ag_ref, head):
    start = head // 2 * LANES
    pair = ag_ref[:, start : start + LANES].astype(F32) * 0.125
    keep = low_half(pair.shape)
    keep = keep if head % 2 == 0 else jnp.logical_not(keep)
    return jnp.where(keep, pair, 0.0).astype(BF16)


def split_agents(ag_ref, heads_ref):
    for head in range(HEADS):
        heads_ref[head, :, :] = head_agents(ag_ref, head)


def project_values(x_ref, w_ref, out_ref):
    rows, width, dim = out_ref.shape
    chunk = 256
    for c in range(0, x_ref.shape[0], chunk):
        y = jnp.dot(x_ref[c : c + chunk, :], w_ref[...], preferred_element_type=F32).astype(BF16)
        for r in range(chunk // width):
            out_ref[c // width + r, :, :] = y[r * width : (r + 1) * width, :]


def project_keys(x_ref, w_ref, out_ref, v_ref, vt_ref):
    rows, width, dim = v_ref.shape
    chunk = 256
    for c in range(0, x_ref.shape[0], chunk):
        y = jnp.dot(x_ref[c : c + chunk, :], w_ref[...], preferred_element_type=F32).astype(BF16)
        for r in range(c // width, (c + chunk) // width):
            vt_ref[:, :, r * width : (r + 1) * width] = v_ref[r].T.reshape(HEADS, dim // HEADS, width)
        for block in range(out_ref.shape[0]):
            out_ref[block, c : c + chunk, :] = y[:, block * LANES : (block + 1) * LANES]


def token_bias(tissue_ref, bias_ref):
    rows, width = tissue_ref.shape
    for r in range(rows):
        bias = jnp.where(tissue_ref[r : r + 1, :] > 0, 0.0, NONE)
        bias_ref[r * width : (r + 1) * width, :] = jnp.broadcast_to(bias, (LANES, width)).T


def score_chunk(pair, side, c, chunk, bias_ref, heads_ref, k_ref, score_ref, slot, top):
    agents = heads_ref.shape[1]
    s = lax.dot_general(
        k_ref[pair, c : c + chunk, :], heads_ref[2 * pair + side], NT, preferred_element_type=F32
    )
    bias = bias_ref[c : c + chunk, :]
    s = s + jnp.concatenate([bias] * (agents // LANES), axis=1)
    score_ref[slot, side, c : c + chunk, :] = s
    return jnp.maximum(top, jnp.max(s.reshape(chunk // 8, 8, agents), axis=0))


def weigh_chunk(head, side, c, chunk, vt_ref, score_ref, slot, top, total, got):
    agents = score_ref.shape[3]
    e = jnp.exp(score_ref[slot, side, c : c + chunk, :] - top)
    total = total + jnp.sum(e.reshape(chunk // 8, 8, agents), axis=0)
    part = jnp.dot(vt_ref[head, :, c : c + chunk], e.astype(BF16), preferred_element_type=F32)
    return total, part if got is None else got + part


def band_stats(after, before, bias_ref, heads_ref, k_ref, vt_ref, score_ref, w_ref, mt_ref, slot, tops):
    tokens = k_ref.shape[1]
    agents = heads_ref.shape[1]
    chunk = 256
    found = []
    for side in range(2):
        top = jnp.full((8, agents), NONE, F32)
        total, got = jnp.zeros((8, agents), F32), None
        if before is not None:
            head = 2 * before + side
            peak = jnp.maximum(tops[side], 0.1 * NONE)
        for c in range(0, tokens, chunk):
            if after is not None:
                top = score_chunk(after, side, c, chunk, bias_ref, heads_ref, k_ref, score_ref, slot, top)
            if before is not None:
                total, got = weigh_chunk(head, side, c, chunk, vt_ref, score_ref, 1 - slot, peak, total, got)
        found.append(jnp.max(top, axis=0, keepdims=True))
        if before is not None:
            w_ref[head, :, :] = got
            mt_ref[head, 0:1, :] = tops[side]
            mt_ref[head, 1:2, :] = jnp.sum(total, axis=0, keepdims=True)
    return found


def token_side(x_ref, wq_ref, heads_ref, tw_ref):
    tokens = x_ref.shape[0]
    chunk, part = 256, 128

    for c in range(0, tokens, chunk):
        q = jnp.dot(x_ref[c : c + chunk, :], wq_ref[...], preferred_element_type=F32).astype(BF16)
        for head in range(HEADS):
            start = head // 2 * LANES
            for p in range(0, chunk, part):
                s = lax.dot_general(
                    heads_ref[head], q[p : p + part, start : start + LANES], NT, preferred_element_type=F32
                )
                e = jnp.exp(s - jnp.max(s, axis=0, keepdims=True))
                share = 1.0 / jnp.sum(e, axis=0, keepdims=True)
                tw_ref[head, :, c + p : c + p + part] = (e * share).astype(BF16)


POINTS = (1.0, -1.0, 2.0, -2.0, 0.5, -0.5)
NORMS = (-4.5, 4.5, 45.0, -45.0, 2.8125, -2.8125)
PLANES = 13


def spread_taps(k7_ref, k5_ref, k3_ref, sum_ref, taps_ref):
    for p in range(7):
        sum_ref[p, 0:7, :] = k7_ref[p]
    for p in range(5):
        sum_ref[p + 1, 1:6, :] = sum_ref[p + 1, 1:6, :] + k5_ref[p]
    for p in range(3):
        sum_ref[p + 2, 2:5, :] = sum_ref[p + 2, 2:5, :] + k3_ref[p]

    def one(block, carry):
        at = pl.ds(pl.multiple_of(block * LANES, LANES), LANES)
        g = [sum_ref[p, 0:7, at] for p in range(7)]
        planes = []
        for first, count in ((0, 4), (4, 3)):
            for point, norm in zip(POINTS, NORMS):
                total = g[first] * (1.0 / norm)
                for j in range(1, count):
                    total = total + g[first + j] * (point**j / norm)
                planes.append(total)
        planes.append(g[3])
        for i, plane in enumerate(planes):
            for q in range(7):
                taps_ref[block, i * 7 + q, :, :] = jnp.broadcast_to(plane[q : q + 1], (8, LANES))
        return carry

    lax.fori_loop(0, taps_ref.shape[0], one, 0)


def fill_sides(ext_ref):
    blocks, planes, padded, _ = ext_ref.shape
    for block in range(blocks):
        for r in range(planes):
            ext_ref[block, r, 0:8, :] = jnp.zeros((8, LANES), F32)
            ext_ref[block, r, padded - 8 : padded, :] = jnp.zeros((8, LANES), F32)


def at_points(d, last):
    planes = []
    e, o = d[0] + d[4] - 4.25 * d[2], d[1] + d[5] - 4.25 * d[3]
    planes += [o + e, o - e]
    e, o = 0.5 * d[0] - 2.5 * d[2] + 2.0 * d[4], 0.25 * d[1] - 1.25 * d[3] + d[5]
    planes += [o + e, o - e]
    e, o = 2.0 * d[0] - 2.5 * d[2] + 0.5 * d[4], 4.0 * d[1] - 5.0 * d[3] + d[5]
    planes += [o + e, o - e]
    if last:
        planes.append(d[6] - d[0] + 5.25 * (d[2] - d[4]))
    return planes


def transform(v_ref, above_ref, below_ref, ext_ref):
    blocks = ext_ref.shape[0]
    rows, width, _ = v_ref.shape
    step = 16

    def one(block, carry):
        at = pl.ds(pl.multiple_of(block * LANES, LANES), LANES)
        for c in range(0, width, step):
            where = slice(c, c + step)
            d = [above_ref[r, where, at].astype(F32) for r in range(3)]
            d += [v_ref[r, where, at].astype(F32) for r in range(rows)]
            d += [below_ref[r, where, at].astype(F32) for r in range(3)]
            planes = at_points(d[0:7], True) + at_points(d[4:11], True) + at_points(d[8:14], False)
            for i, plane in enumerate(planes):
                ext_ref[block, i, c + 8 : c + 8 + step, :] = plane
        return carry

    lax.fori_loop(0, blocks, one, 0)


def convolve(ext_ref, taps_ref, pos_ref, first, last):
    width = pos_ref.shape[2]
    step = 16

    def one(block, carry):
        for c in range(0, width, step):
            sums = [[None] * 7, [None] * 7]
            for q in range(7):
                x = [ext_ref[block, i, c + 5 + q : c + 5 + q + step, :] for i in range(20)]
                for k in range(PLANES):
                    tap = taps_ref[block, k * 7 + q]
                    tap = jnp.concatenate([tap] * (step // 8), axis=0)
                    point, group = (6, 0) if k == 12 else (k % 6, k // 6)
                    for tile in range(2):
                        term = x[(group + tile) * 7 + point] * tap
                        old = sums[tile][point]
                        sums[tile][point] = term if old is None else old + term
            for tile in range(2):
                m = sums[tile]
                s1, d1 = m[0] + m[1], m[0] - m[1]
                s2, d2 = m[2] + m[3], m[2] - m[3]
                s3, d3 = m[4] + m[5], m[4] - m[5]
                outs = (
                    s1 + s2 + s3,
                    d1 + 2.0 * d2 + 0.5 * d3,
                    s1 + 4.0 * s2 + 0.25 * s3,
                    d1 + 8.0 * d2 + 0.125 * d3 + m[6],
                )
                for i, y in enumerate(outs):
                    pos_ref[block, tile * 4 + i, c : c + step, :] = y
        return carry

    lax.fori_loop(first, last, one, 0)


def blend(av_t, tw_ref, pos_ref, out_ref):
    blocks, _, width, _ = pos_ref.shape
    chunk = 256
    for c in range(0, out_ref.shape[0], chunk):
        parts = []
        for head in range(HEADS):
            parts.append(
                jnp.dot(
                    av_t[head * 64 : head * 64 + 64, :],
                    tw_ref[head, :, c : c + chunk],
                    preferred_element_type=F32,
                )
            )
        attended = jnp.concatenate(parts, axis=0).T
        position = jnp.concatenate(
            [
                jnp.concatenate([pos_ref[b, r] for b in range(blocks)], axis=1)
                for r in range(c // width, (c + chunk) // width)
            ],
            axis=0,
        )
        out_ref[c : c + chunk, :] = (attended + position).astype(BF16)


class Exchange:
    def __init__(self, n, v_ref, refs, sems):
        self.n, self.me = n, lax.axis_index("col")
        (self.w, self.mt, self.wp, self.mtp, self.ws, self.ms, self.wr, self.mr, self.av,
         above_ref, below_ref) = refs
        s1, r1, s2, r2, s3, r3, s4, r4 = sems
        me, m = self.me, n // 2
        self.m = m
        self.low, self.group = lax.rem(me, 2), me // 2
        twin = me + 1 - 2 * self.low
        self.to = [lax.rem(me + k, n) for k in range(1, n)]
        rows = v_ref.shape[0]
        half = HEADS // 2
        self.mine, self.other = half * self.low, half * (1 - self.low)

        def remote(src, dst, s, r, peer):
            return pltpu.make_async_remote_copy(
                src_ref=src, dst_ref=dst, send_sem=s, recv_sem=r,
                device_id={"col": peer}, device_id_type=pl.DeviceIdType.MESH,
            )

        self.swap = [
            remote(self.w.at[pl.ds(self.other, half)], self.wp, s1.at[0], r1.at[0], twin),
            remote(self.mt.at[pl.ds(self.other, half)], self.mtp, s1.at[1], r1.at[1], twin),
        ]
        self.scatter = []
        self.crossing = []
        for k in range(1, m):
            g = lax.rem(self.group + k, m)
            peer = 2 * g + self.low
            group = self.crossing if k % 2 else self.scatter
            group.append(remote(self.ws.at[g], self.wr.at[self.group], s2.at[0, k - 1], r2.at[0, k - 1], peer))
            group.append(remote(self.ms.at[g], self.mr.at[self.group], s2.at[1, k - 1], r2.at[1, k - 1], peer))
        self.slot = m * self.low + self.group
        self.gather = []
        for k in range(1, m):
            peer = 2 * lax.rem(self.group + k, m) + self.low
            self.gather.append(
                remote(self.av.at[self.slot], self.av.at[self.slot], s4.at[k - 1], r4.at[k - 1], peer)
            )
        own = self.av.at[pl.ds(m * self.low, m)]
        self.forward = remote(own, own, s4.at[m - 1], r4.at[m - 1], twin)
        self.down = remote(v_ref.at[pl.ds(rows - 3, 3)], above_ref, s3.at[0], r3.at[0], lax.rem(me + 1, n))
        self.up = remote(v_ref.at[pl.ds(0, 3)], below_ref, s3.at[1], r3.at[1], lax.rem(me + n - 1, n))

    def greet(self):
        barrier = pltpu.get_barrier_semaphore()
        for p in self.to:
            pl.semaphore_signal(
                barrier, inc=1, device_id={"col": p}, device_id_type=pl.DeviceIdType.MESH
            )

    def met(self):
        pl.semaphore_wait(pltpu.get_barrier_semaphore(), self.n - 1)

    def send_rims(self):
        @pl.when(self.me < self.n - 1)
        def _():
            self.down.start()

        @pl.when(self.me > 0)
        def _():
            self.up.start()

    def send_twin(self):
        for copy in self.swap:
            copy.start()

    def merge(self):
        for copy in self.swap:
            copy.wait()
        half, depth, _ = self.wp.shape
        piece = self.ws.shape[1]
        for h in range(half):
            a, b = self.mt[self.mine + h], self.mtp[h]
            top = jnp.maximum(a[0:1], b[0:1])
            fa, fb = jnp.exp(a[0:1] - top), jnp.exp(b[0:1] - top)
            total = a[1:2] * fa + b[1:2] * fb
            w = self.w[self.mine + h] * fa + self.wp[h] * fb
            for p in range(depth // piece):
                at = h * depth // piece + p
                self.ws[at] = w[p * piece : (p + 1) * piece]
                self.ms[at, 0:1, :] = top
                self.ms[at, 1:2, :] = total
        for copy in self.scatter + self.crossing:
            copy.start()
        self.wr[self.group] = self.ws[self.group]
        self.mr[self.group] = self.ms[self.group]

    def cross(self):
        for copy in self.crossing:
            copy.start()

    def reduce(self):
        for copy in self.scatter + self.crossing:
            copy.wait()
        tops = [self.mr[i, 0:1, :] for i in range(self.m)]
        top = functools.reduce(jnp.maximum, tops)
        total, weighted = 0.0, 0.0
        for i in range(self.m):
            f = jnp.exp(tops[i] - top)
            total = total + f * self.mr[i, 1:2, :]
            weighted = weighted + f * self.wr[i]
        self.av[self.slot] = (weighted / total).astype(BF16)
        for copy in self.gather:
            copy.start()

    def rims(self):
        @pl.when(self.me < self.n - 1)
        def _():
            self.down.wait_send()
            self.up.wait_recv()

        @pl.when(self.me > 0)
        def _():
            self.down.wait_recv()
            self.up.wait_send()

    def pass_on(self):
        for copy in self.gather:
            copy.wait()
        self.forward.start()

    def end(self):
        self.forward.wait()


def sem_shapes(n):
    dma = pltpu.SemaphoreType.DMA
    m = n // 2
    return [dma((2,)), dma((2,)), dma((2, m - 1)), dma((2, m - 1)), dma((2,)), dma((2,)),
            dma((m,)), dma((m,))]


def whole_kernel(n, *refs):
    sources, out_ref = refs[:9], refs[9]
    held, load_sem = refs[10:19], refs[19]
    x_ref, tissue_ref, wq_ref, wk_ref, wv_ref, ag_ref, k7_ref, k5_ref, k3_ref = held
    (v_ref, vt_ref, k_ref, bias_ref, score_ref, tw_ref, sum_ref, taps_ref, ext_ref, pos_ref, heads_ref) = refs[20:31]
    shared, sems = refs[31:42], refs[42:]
    w_ref, mt_ref, av_ref, above_ref, below_ref = shared[0], shared[1], shared[8], shared[9], shared[10]
    loads = [pltpu.make_async_copy(sources[i], held[i], load_sem.at[i]) for i in range(9)]
    for i in (5, 1, 0, 4, 3, 2, 6, 7, 8):
        loads[i].start()
    work = Exchange(n, v_ref, shared, sems)

    @pl.when(work.me == 0)
    def _():
        above_ref[...] = jnp.zeros(above_ref.shape, BF16)

    @pl.when(work.me == n - 1)
    def _():
        below_ref[...] = jnp.zeros(below_ref.shape, BF16)

    work.greet()
    loads[5].wait()
    split_agents(ag_ref, heads_ref)
    loads[1].wait()
    token_bias(tissue_ref, bias_ref)
    loads[0].wait()
    loads[4].wait()
    project_values(x_ref, wv_ref, v_ref)
    loads[3].wait()
    project_keys(x_ref, wk_ref, k_ref, v_ref, vt_ref)
    work.met()
    work.send_rims()

    def stats(after, before, slot, tops):
        return band_stats(
            after, before, bias_ref, heads_ref, k_ref, vt_ref, score_ref, w_ref, mt_ref, slot, tops
        )

    order = [work.other // 2 + i for i in range(HEADS // 4)] + [work.mine // 2 + i for i in range(HEADS // 4)]
    tops = None
    for i in range(HEADS // 2 + 1):
        after = order[i] if i < HEADS // 2 else None
        before = order[i - 1] if i > 0 else None
        tops = stats(after, before, i % 2, tops)
        if i == HEADS // 4:
            work.send_twin()
    work.merge()
    for i in (6, 7, 8, 2):
        loads[i].wait()
    fill_sides(ext_ref)
    spread_taps(k7_ref, k5_ref, k3_ref, sum_ref, taps_ref)
    token_side(x_ref, wq_ref, heads_ref, tw_ref)
    work.rims()
    transform(v_ref, above_ref, below_ref, ext_ref)
    blocks = pos_ref.shape[0]
    work.reduce()
    convolve(ext_ref, taps_ref, pos_ref, 0, 3)
    work.pass_on()
    convolve(ext_ref, taps_ref, pos_ref, 3, 4)
    work.end()
    av_t = jnp.concatenate([av_ref[i] for i in range(n)], axis=0)
    blend(av_t, tw_ref, pos_ref, out_ref)


def on_device(n, patches, tissue, w_query, w_key, w_value, w_out, agent_tokens, k7, k5, k3):
    rows, width, dim = patches.shape
    tokens = rows * width
    agents = agent_tokens.shape[0]
    x = patches.reshape(tokens, dim)
    rim = (3, width, dim)
    blocks = dim // LANES
    depth, half, m = dim // HEADS, HEADS // 2, n // 2
    piece = dim // n
    given = (x, tissue, w_query, w_key, w_value, agent_tokens, k7, k5, k3)
    blended = pl.pallas_call(
        functools.partial(whole_kernel, n),
        out_shape=pltpu.VMEM((tokens, dim), BF16),
        in_specs=[pl.BlockSpec(memory_space=pltpu.HBM)] * len(given),
        out_specs=VMEM,
        scratch_shapes=[pltpu.VMEM(a.shape, a.dtype) for a in given]
        + [
            pltpu.SemaphoreType.DMA((len(given),)),
            pltpu.VMEM((rows, width, dim), BF16),
            pltpu.VMEM((HEADS, depth, tokens), BF16),
            pltpu.VMEM((blocks, tokens, LANES), BF16),
            pltpu.VMEM((tokens, LANES), F32),
            pltpu.VMEM((2, 2, tokens, agents), F32),
            pltpu.VMEM((HEADS, agents, tokens), BF16),
            pltpu.VMEM((7, 8, dim), F32),
            pltpu.VMEM((blocks, 7 * PLANES, 8, LANES), F32),
            pltpu.VMEM((blocks, 20, width + 16, LANES), F32),
            pltpu.VMEM((blocks, rows, width, LANES), F32),
            pltpu.VMEM((HEADS, agents, LANES), BF16),
            pltpu.VMEM((HEADS, depth, agents), F32),
            pltpu.VMEM((HEADS, 2, agents), F32),
            pltpu.VMEM((half, depth, agents), F32),
            pltpu.VMEM((half, 2, agents), F32),
            pltpu.VMEM((m, piece, agents), F32),
            pltpu.VMEM((m, 2, agents), F32),
            pltpu.VMEM((m, piece, agents), F32),
            pltpu.VMEM((m, 2, agents), F32),
            pltpu.VMEM((n, piece, agents), BF16),
            pltpu.VMEM(rim, BF16),
            pltpu.VMEM(rim, BF16),
        ]
        + sem_shapes(n),
        compiler_params=pltpu.CompilerParams(
            vmem_limit_bytes=LIMIT, collective_id=0, has_side_effects=True
        ),
    )(*given)
    mixed = jnp.dot(blended, w_out, preferred_element_type=F32).astype(BF16)
    return mixed.reshape(rows, width, dim)


def solution(mesh):
    rows = P(("slide", "col"), None, None)
    return jax.shard_map(
        functools.partial(on_device, mesh.shape["col"]),
        mesh=mesh,
        in_specs=(rows, P(("slide", "col"), None)) + (P(),) * 8,
        out_specs=rows,
        check_vma=False,
    )
```

```python
import functools

import jax
import jax.numpy as jnp
from jax import lax
from jax.experimental import pallas as pl
from jax.experimental.pallas import tpu as pltpu
from jax.sharding import PartitionSpec as P

HEADS = 8
LANES = 128
NONE = -1e30
F32, BF16 = jnp.float32, jnp.bfloat16
NT = (((1,), (1,)), ((), ()))
VMEM = pl.BlockSpec(memory_space=pltpu.VMEM)
LIMIT = 56 * 1024 * 1024


def low_half(shape):
    return lax.broadcasted_iota(jnp.int32, shape, len(shape) - 1) < LANES // 2


def head_agents(ag_ref, head):
    start = head // 2 * LANES
    pair = ag_ref[:, start : start + LANES].astype(F32) * 0.125
    keep = low_half(pair.shape)
    keep = keep if head % 2 == 0 else jnp.logical_not(keep)
    return jnp.where(keep, pair, 0.0).astype(BF16)


def split_agents(ag_ref, heads_ref):
    for head in range(HEADS):
        heads_ref[head, :, :] = head_agents(ag_ref, head)


def project_values(x_ref, w_ref, out_ref):
    rows, width, dim = out_ref.shape
    chunk = 256
    for c in range(0, x_ref.shape[0], chunk):
        y = jnp.dot(x_ref[c : c + chunk, :], w_ref[...], preferred_element_type=F32).astype(BF16)
        for r in range(chunk // width):
            out_ref[c // width + r, :, :] = y[r * width : (r + 1) * width, :]


def project_keys(x_ref, w_ref, out_ref, v_ref, vt_ref):
    rows, width, dim = v_ref.shape
    chunk = 256
    for c in range(0, x_ref.shape[0], chunk):
        y = jnp.dot(x_ref[c : c + chunk, :], w_ref[...], preferred_element_type=F32).astype(BF16)
        for r in range(c // width, (c + chunk) // width):
            vt_ref[:, :, r * width : (r + 1) * width] = v_ref[r].T.reshape(HEADS, dim // HEADS, width)
        for block in range(out_ref.shape[0]):
            out_ref[block, c : c + chunk, :] = y[:, block * LANES : (block + 1) * LANES]


def token_bias(tissue_ref, bias_ref):
    rows, width = tissue_ref.shape
    for r in range(rows):
        bias = jnp.where(tissue_ref[r : r + 1, :] > 0, 0.0, NONE)
        bias_ref[r * width : (r + 1) * width, :] = jnp.broadcast_to(bias, (LANES, width)).T


def score_chunk(pair, side, c, chunk, bias_ref, heads_ref, k_ref, score_ref, slot, top):
    agents = heads_ref.shape[1]
    s = lax.dot_general(
        k_ref[pair, c : c + chunk, :], heads_ref[2 * pair + side], NT, preferred_element_type=F32
    )
    bias = bias_ref[c : c + chunk, :]
    s = s + jnp.concatenate([bias] * (agents // LANES), axis=1)
    score_ref[slot, side, c : c + chunk, :] = s
    return jnp.maximum(top, jnp.max(s.reshape(chunk // 8, 8, agents), axis=0))


def weigh_chunk(head, side, c, chunk, vt_ref, score_ref, slot, top, total, got):
    agents = score_ref.shape[3]
    e = jnp.exp(score_ref[slot, side, c : c + chunk, :] - top)
    total = total + jnp.sum(e.reshape(chunk // 8, 8, agents), axis=0)
    part = jnp.dot(vt_ref[head, :, c : c + chunk], e.astype(BF16), preferred_element_type=F32)
    return total, part if got is None else got + part


def band_stats(after, before, bias_ref, heads_ref, k_ref, vt_ref, score_ref, w_ref, mt_ref, slot, tops):
    tokens = k_ref.shape[1]
    agents = heads_ref.shape[1]
    chunk = 256
    found = []
    for side in range(2):
        top = jnp.full((8, agents), NONE, F32)
        total, got = jnp.zeros((8, agents), F32), None
        if before is not None:
            head = 2 * before + side
            peak = jnp.maximum(tops[side], 0.1 * NONE)
        for c in range(0, tokens, chunk):
            if after is not None:
                top = score_chunk(after, side, c, chunk, bias_ref, heads_ref, k_ref, score_ref, slot, top)
            if before is not None:
                total, got = weigh_chunk(head, side, c, chunk, vt_ref, score_ref, 1 - slot, peak, total, got)
        found.append(jnp.max(top, axis=0, keepdims=True))
        if before is not None:
            w_ref[head, :, :] = got
            mt_ref[head, 0:1, :] = tops[side]
            mt_ref[head, 1:2, :] = jnp.sum(total, axis=0, keepdims=True)
    return found


def token_side(x_ref, wq_ref, heads_ref, tw_ref):
    tokens = x_ref.shape[0]
    chunk, part = 256, 128

    for c in range(0, tokens, chunk):
        q = jnp.dot(x_ref[c : c + chunk, :], wq_ref[...], preferred_element_type=F32).astype(BF16)
        for head in range(HEADS):
            start = head // 2 * LANES
            for p in range(0, chunk, part):
                s = lax.dot_general(
                    heads_ref[head], q[p : p + part, start : start + LANES], NT, preferred_element_type=F32
                )
                e = jnp.exp(s - jnp.max(s, axis=0, keepdims=True))
                share = 1.0 / jnp.sum(e, axis=0, keepdims=True)
                tw_ref[head, :, c + p : c + p + part] = (e * share).astype(BF16)


POINTS = (1.0, -1.0, 2.0, -2.0, 0.5, -0.5)
NORMS = (-4.5, 4.5, 45.0, -45.0, 2.8125, -2.8125)
PLANES = 13


def spread_taps(k7_ref, k5_ref, k3_ref, sum_ref, taps_ref):
    for p in range(7):
        sum_ref[p, 0:7, :] = k7_ref[p]
    for p in range(5):
        sum_ref[p + 1, 1:6, :] = sum_ref[p + 1, 1:6, :] + k5_ref[p]
    for p in range(3):
        sum_ref[p + 2, 2:5, :] = sum_ref[p + 2, 2:5, :] + k3_ref[p]

    def one(block, carry):
        at = pl.ds(pl.multiple_of(block * LANES, LANES), LANES)
        g = [sum_ref[p, 0:7, at] for p in range(7)]
        planes = []
        for first, count in ((0, 4), (4, 3)):
            for point, norm in zip(POINTS, NORMS):
                total = g[first] * (1.0 / norm)
                for j in range(1, count):
                    total = total + g[first + j] * (point**j / norm)
                planes.append(total)
        planes.append(g[3])
        for i, plane in enumerate(planes):
            for q in range(7):
                taps_ref[block, i * 7 + q, :, :] = jnp.broadcast_to(plane[q : q + 1], (8, LANES))
        return carry

    lax.fori_loop(0, taps_ref.shape[0], one, 0)


def fill_sides(ext_ref):
    blocks, planes, padded, _ = ext_ref.shape
    for block in range(blocks):
        for r in range(planes):
            ext_ref[block, r, 0:8, :] = jnp.zeros((8, LANES), F32)
            ext_ref[block, r, padded - 8 : padded, :] = jnp.zeros((8, LANES), F32)


def at_points(d, last):
    planes = []
    e, o = d[0] + d[4] - 4.25 * d[2], d[1] + d[5] - 4.25 * d[3]
    planes += [o + e, o - e]
    e, o = 0.5 * d[0] - 2.5 * d[2] + 2.0 * d[4], 0.25 * d[1] - 1.25 * d[3] + d[5]
    planes += [o + e, o - e]
    e, o = 2.0 * d[0] - 2.5 * d[2] + 0.5 * d[4], 4.0 * d[1] - 5.0 * d[3] + d[5]
    planes += [o + e, o - e]
    if last:
        planes.append(d[6] - d[0] + 5.25 * (d[2] - d[4]))
    return planes


def transform_own(v_ref, ext_ref):
    rows, width, _ = v_ref.shape
    step = 16

    def one(block, carry):
        at = pl.ds(pl.multiple_of(block * LANES, LANES), LANES)
        for c in range(0, width, step):
            where = slice(c, c + step)
            d = [v_ref[r, where, at].astype(F32) for r in range(1, rows)]
            for i, plane in enumerate(at_points(d, True)):
                ext_ref[block, 7 + i, c + 8 : c + 8 + step, :] = plane
        return carry

    lax.fori_loop(0, ext_ref.shape[0], one, 0)


def transform_rims(v_ref, above_ref, below_ref, ext_ref):
    rows, width, _ = v_ref.shape
    step = 16

    def one(block, carry):
        at = pl.ds(pl.multiple_of(block * LANES, LANES), LANES)
        for c in range(0, width, step):
            where = slice(c, c + step)
            d = [above_ref[r, where, at].astype(F32) for r in range(3)]
            d += [v_ref[r, where, at].astype(F32) for r in range(4)]
            for i, plane in enumerate(at_points(d, True)):
                ext_ref[block, i, c + 8 : c + 8 + step, :] = plane
            d = [v_ref[r, where, at].astype(F32) for r in range(rows - 3, rows)]
            d += [below_ref[r, where, at].astype(F32) for r in range(3)]
            for i, plane in enumerate(at_points(d, False)):
                ext_ref[block, 14 + i, c + 8 : c + 8 + step, :] = plane
        return carry

    lax.fori_loop(0, ext_ref.shape[0], one, 0)


def wide_tap(taps_ref, block, plane, q, step):
    return jnp.concatenate([taps_ref[block, plane * 7 + q]] * (step // 8), axis=0)


def convolve_own(ext_ref, taps_ref, part_ref):
    blocks, _, width, _ = part_ref.shape
    step = 16

    def one(block, carry):
        for c in range(0, width, step):
            sums = [None] * PLANES
            for q in range(7):
                for point in range(7):
                    x = ext_ref[block, 7 + point, c + 5 + q : c + 5 + q + step, :]
                    for tile, plane in ((0, 6 + point), (1, point if point < 6 else 12)):
                        if tile == 0 and point == 6:
                            continue
                        term = x * wide_tap(taps_ref, block, plane, q, step)
                        at = 6 * tile + point
                        sums[at] = term if sums[at] is None else sums[at] + term
            for i, total in enumerate(sums):
                part_ref[block, i, c : c + step, :] = total
        return carry

    lax.fori_loop(0, blocks, one, 0)


def convolve(ext_ref, taps_ref, part_ref, pos_ref, first, last):
    width = pos_ref.shape[2]
    step = 16

    def one(block, carry):
        for c in range(0, width, step):
            here = slice(c, c + step)
            m = [
                [part_ref[block, i, here, :] for i in range(6)] + [None],
                [part_ref[block, 6 + i, here, :] for i in range(7)],
            ]
            for q in range(7):
                where = slice(c + 5 + q, c + 5 + q + step)
                for point in range(7):
                    tap = wide_tap(taps_ref, block, point if point < 6 else 12, q, step)
                    term = ext_ref[block, point, where, :] * tap
                    m[0][point] = term if m[0][point] is None else m[0][point] + term
                for point in range(6):
                    tap = wide_tap(taps_ref, block, 6 + point, q, step)
                    m[1][point] = m[1][point] + ext_ref[block, 14 + point, where, :] * tap
            for tile in range(2):
                a = m[tile]
                s1, d1 = a[0] + a[1], a[0] - a[1]
                s2, d2 = a[2] + a[3], a[2] - a[3]
                s3, d3 = a[4] + a[5], a[4] - a[5]
                outs = (
                    s1 + s2 + s3,
                    d1 + 2.0 * d2 + 0.5 * d3,
                    s1 + 4.0 * s2 + 0.25 * s3,
                    d1 + 8.0 * d2 + 0.125 * d3 + a[6],
                )
                for i, y in enumerate(outs):
                    pos_ref[block, tile * 4 + i, here, :] = y
        return carry

    lax.fori_loop(first, last, one, 0)


def blend(av_t, tw_ref, pos_ref, out_ref):
    blocks, _, width, _ = pos_ref.shape
    chunk = 256
    for c in range(0, out_ref.shape[0], chunk):
        parts = []
        for head in range(HEADS):
            parts.append(
                jnp.dot(
                    av_t[head * 64 : head * 64 + 64, :],
                    tw_ref[head, :, c : c + chunk],
                    preferred_element_type=F32,
                )
            )
        attended = jnp.concatenate(parts, axis=0).T
        position = jnp.concatenate(
            [
                jnp.concatenate([pos_ref[b, r] for b in range(blocks)], axis=1)
                for r in range(c // width, (c + chunk) // width)
            ],
            axis=0,
        )
        out_ref[c : c + chunk, :] = (attended + position).astype(BF16)


class Exchange:
    def __init__(self, n, v_ref, refs, sems):
        self.n, self.me = n, lax.axis_index("col")
        (self.w, self.mt, self.wp, self.mtp, self.ws, self.ms, self.wr, self.mr, self.av,
         above_ref, below_ref) = refs
        s1, r1, s2, r2, s3, r3, s4, r4 = sems
        me, m = self.me, n // 2
        self.m = m
        self.low, self.group = lax.rem(me, 2), me // 2
        twin = me + 1 - 2 * self.low
        self.to = [lax.rem(me + k, n) for k in range(1, n)]
        rows = v_ref.shape[0]
        half = HEADS // 2
        self.mine, self.other = half * self.low, half * (1 - self.low)

        def remote(src, dst, s, r, peer):
            return pltpu.make_async_remote_copy(
                src_ref=src, dst_ref=dst, send_sem=s, recv_sem=r,
                device_id={"col": peer}, device_id_type=pl.DeviceIdType.MESH,
            )

        self.swap = [
            remote(self.w.at[pl.ds(self.other, half)], self.wp, s1.at[0], r1.at[0], twin),
            remote(self.mt.at[pl.ds(self.other, half)], self.mtp, s1.at[1], r1.at[1], twin),
        ]
        self.scatter = []
        self.crossing = []
        for k in range(1, m):
            g = lax.rem(self.group + k, m)
            peer = 2 * g + self.low
            group = self.crossing if k % 2 else self.scatter
            group.append(remote(self.ws.at[g], self.wr.at[self.group], s2.at[0, k - 1], r2.at[0, k - 1], peer))
            group.append(remote(self.ms.at[g], self.mr.at[self.group], s2.at[1, k - 1], r2.at[1, k - 1], peer))
        self.slot = m * self.low + self.group
        self.gather = []
        for k in range(1, m):
            peer = 2 * lax.rem(self.group + k, m) + self.low
            self.gather.append(
                remote(self.av.at[self.slot], self.av.at[self.slot], s4.at[k - 1], r4.at[k - 1], peer)
            )
        own = self.av.at[pl.ds(m * self.low, m)]
        self.forward = remote(own, own, s4.at[m - 1], r4.at[m - 1], twin)
        self.down = remote(v_ref.at[pl.ds(rows - 3, 3)], above_ref, s3.at[0], r3.at[0], lax.rem(me + 1, n))
        self.up = remote(v_ref.at[pl.ds(0, 3)], below_ref, s3.at[1], r3.at[1], lax.rem(me + n - 1, n))

    def greet(self):
        barrier = pltpu.get_barrier_semaphore()
        for p in self.to:
            pl.semaphore_signal(
                barrier, inc=1, device_id={"col": p}, device_id_type=pl.DeviceIdType.MESH
            )

    def met(self):
        pl.semaphore_wait(pltpu.get_barrier_semaphore(), self.n - 1)

    def send_rims(self):
        @pl.when(self.me < self.n - 1)
        def _():
            self.down.start()

        @pl.when(self.me > 0)
        def _():
            self.up.start()

    def send_twin(self):
        for copy in self.swap:
            copy.start()

    def merge(self):
        for copy in self.swap:
            copy.wait()
        half, depth, _ = self.wp.shape
        piece = self.ws.shape[1]
        for h in range(half):
            a, b = self.mt[self.mine + h], self.mtp[h]
            top = jnp.maximum(a[0:1], b[0:1])
            fa, fb = jnp.exp(a[0:1] - top), jnp.exp(b[0:1] - top)
            total = a[1:2] * fa + b[1:2] * fb
            w = self.w[self.mine + h] * fa + self.wp[h] * fb
            for p in range(depth // piece):
                at = h * depth // piece + p
                self.ws[at] = w[p * piece : (p + 1) * piece]
                self.ms[at, 0:1, :] = top
                self.ms[at, 1:2, :] = total
        for copy in self.scatter + self.crossing:
            copy.start()
        self.wr[self.group] = self.ws[self.group]
        self.mr[self.group] = self.ms[self.group]

    def cross(self):
        for copy in self.crossing:
            copy.start()

    def reduce(self):
        for copy in self.scatter + self.crossing:
            copy.wait()
        tops = [self.mr[i, 0:1, :] for i in range(self.m)]
        top = functools.reduce(jnp.maximum, tops)
        total, weighted = 0.0, 0.0
        for i in range(self.m):
            f = jnp.exp(tops[i] - top)
            total = total + f * self.mr[i, 1:2, :]
            weighted = weighted + f * self.wr[i]
        self.av[self.slot] = (weighted / total).astype(BF16)
        for copy in self.gather:
            copy.start()

    def rims(self):
        @pl.when(self.me < self.n - 1)
        def _():
            self.down.wait_send()
            self.up.wait_recv()

        @pl.when(self.me > 0)
        def _():
            self.down.wait_recv()
            self.up.wait_send()

    def pass_on(self):
        for copy in self.gather:
            copy.wait()
        self.forward.start()

    def end(self):
        self.forward.wait()


def sem_shapes(n):
    dma = pltpu.SemaphoreType.DMA
    m = n // 2
    return [dma((2,)), dma((2,)), dma((2, m - 1)), dma((2, m - 1)), dma((2,)), dma((2,)),
            dma((m,)), dma((m,))]


def whole_kernel(n, *refs):
    sources, out_ref = refs[:9], refs[9]
    held, load_sem = refs[10:19], refs[19]
    x_ref, tissue_ref, wq_ref, wk_ref, wv_ref, ag_ref, k7_ref, k5_ref, k3_ref = held
    (v_ref, vt_ref, k_ref, bias_ref, score_ref, tw_ref, sum_ref, taps_ref, ext_ref, part_ref, pos_ref, heads_ref) = refs[20:32]
    shared, sems = refs[32:43], refs[43:]
    w_ref, mt_ref, av_ref, above_ref, below_ref = shared[0], shared[1], shared[8], shared[9], shared[10]
    loads = [pltpu.make_async_copy(sources[i], held[i], load_sem.at[i]) for i in range(9)]
    for i in (5, 1, 0, 4, 3, 2, 6, 7, 8):
        loads[i].start()
    work = Exchange(n, v_ref, shared, sems)

    @pl.when(work.me == 0)
    def _():
        above_ref[...] = jnp.zeros(above_ref.shape, BF16)

    @pl.when(work.me == n - 1)
    def _():
        below_ref[...] = jnp.zeros(below_ref.shape, BF16)

    work.greet()
    loads[5].wait()
    split_agents(ag_ref, heads_ref)
    loads[1].wait()
    token_bias(tissue_ref, bias_ref)
    loads[0].wait()
    loads[4].wait()
    project_values(x_ref, wv_ref, v_ref)
    loads[3].wait()
    project_keys(x_ref, wk_ref, k_ref, v_ref, vt_ref)
    work.met()
    work.send_rims()

    def stats(after, before, slot, tops):
        return band_stats(
            after, before, bias_ref, heads_ref, k_ref, vt_ref, score_ref, w_ref, mt_ref, slot, tops
        )

    order = [work.other // 2 + i for i in range(HEADS // 4)] + [work.mine // 2 + i for i in range(HEADS // 4)]
    tops = None
    for i in range(HEADS // 2 + 1):
        after = order[i] if i < HEADS // 2 else None
        before = order[i - 1] if i > 0 else None
        tops = stats(after, before, i % 2, tops)
        if i == HEADS // 4:
            work.send_twin()
    work.merge()
    for i in (6, 7, 8, 2):
        loads[i].wait()
    fill_sides(ext_ref)
    spread_taps(k7_ref, k5_ref, k3_ref, sum_ref, taps_ref)
    transform_own(v_ref, ext_ref)
    token_side(x_ref, wq_ref, heads_ref, tw_ref)
    convolve_own(ext_ref, taps_ref, part_ref)
    blocks = pos_ref.shape[0]
    work.reduce()
    work.rims()
    transform_rims(v_ref, above_ref, below_ref, ext_ref)
    convolve(ext_ref, taps_ref, part_ref, pos_ref, 0, blocks - 1)
    work.pass_on()
    convolve(ext_ref, taps_ref, part_ref, pos_ref, blocks - 1, blocks)
    work.end()
    av_t = jnp.concatenate([av_ref[i] for i in range(n)], axis=0)
    blend(av_t, tw_ref, pos_ref, out_ref)


def on_device(n, patches, tissue, w_query, w_key, w_value, w_out, agent_tokens, k7, k5, k3):
    rows, width, dim = patches.shape
    tokens = rows * width
    agents = agent_tokens.shape[0]
    x = patches.reshape(tokens, dim)
    rim = (3, width, dim)
    blocks = dim // LANES
    depth, half, m = dim // HEADS, HEADS // 2, n // 2
    piece = dim // n
    given = (x, tissue, w_query, w_key, w_value, agent_tokens, k7, k5, k3)
    blended = pl.pallas_call(
        functools.partial(whole_kernel, n),
        out_shape=pltpu.VMEM((tokens, dim), BF16),
        in_specs=[pl.BlockSpec(memory_space=pltpu.HBM)] * len(given),
        out_specs=VMEM,
        scratch_shapes=[pltpu.VMEM(a.shape, a.dtype) for a in given]
        + [
            pltpu.SemaphoreType.DMA((len(given),)),
            pltpu.VMEM((rows, width, dim), BF16),
            pltpu.VMEM((HEADS, depth, tokens), BF16),
            pltpu.VMEM((blocks, tokens, LANES), BF16),
            pltpu.VMEM((tokens, LANES), F32),
            pltpu.VMEM((2, 2, tokens, agents), F32),
            pltpu.VMEM((HEADS, agents, tokens), BF16),
            pltpu.VMEM((7, 8, dim), F32),
            pltpu.VMEM((blocks, 7 * PLANES, 8, LANES), F32),
            pltpu.VMEM((blocks, 20, width + 16, LANES), F32),
            pltpu.VMEM((blocks, PLANES, width, LANES), F32),
            pltpu.VMEM((blocks, rows, width, LANES), F32),
            pltpu.VMEM((HEADS, agents, LANES), BF16),
            pltpu.VMEM((HEADS, depth, agents), F32),
            pltpu.VMEM((HEADS, 2, agents), F32),
            pltpu.VMEM((half, depth, agents), F32),
            pltpu.VMEM((half, 2, agents), F32),
            pltpu.VMEM((m, piece, agents), F32),
            pltpu.VMEM((m, 2, agents), F32),
            pltpu.VMEM((m, piece, agents), F32),
            pltpu.VMEM((m, 2, agents), F32),
            pltpu.VMEM((n, piece, agents), BF16),
            pltpu.VMEM(rim, BF16),
            pltpu.VMEM(rim, BF16),
        ]
        + sem_shapes(n),
        compiler_params=pltpu.CompilerParams(
            vmem_limit_bytes=LIMIT, collective_id=0, has_side_effects=True
        ),
    )(*given)
    mixed = jnp.dot(blended, w_out, preferred_element_type=F32).astype(BF16)
    return mixed.reshape(rows, width, dim)


def solution(mesh):
    rows = P(("slide", "col"), None, None)
    return jax.shard_map(
        functools.partial(on_device, mesh.shape["col"]),
        mesh=mesh,
        in_specs=(rows, P(("slide", "col"), None)) + (P(),) * 8,
        out_specs=rows,
        check_vma=False,
    )
```

```python
import functools

import jax
import jax.numpy as jnp
from jax import lax
from jax.experimental import pallas as pl
from jax.experimental.pallas import tpu as pltpu
from jax.sharding import PartitionSpec as P

HEADS = 8
LANES = 128
NONE = -1e30
F32, BF16 = jnp.float32, jnp.bfloat16
NT = (((1,), (1,)), ((), ()))
VMEM = pl.BlockSpec(memory_space=pltpu.VMEM)
LIMIT = 56 * 1024 * 1024


def low_half(shape):
    return lax.broadcasted_iota(jnp.int32, shape, len(shape) - 1) < LANES // 2


def head_agents(ag_ref, head):
    start = head // 2 * LANES
    pair = ag_ref[:, start : start + LANES].astype(F32) * 0.125
    keep = low_half(pair.shape)
    keep = keep if head % 2 == 0 else jnp.logical_not(keep)
    return jnp.where(keep, pair, 0.0).astype(BF16)


def split_agents(ag_ref, heads_ref):
    for head in range(HEADS):
        heads_ref[head, :, :] = head_agents(ag_ref, head)


def project_values(x_ref, w_ref, out_ref):
    rows, width, dim = out_ref.shape
    chunk = 256
    for c in range(0, x_ref.shape[0], chunk):
        y = jnp.dot(x_ref[c : c + chunk, :], w_ref[...], preferred_element_type=F32).astype(BF16)
        for r in range(chunk // width):
            out_ref[c // width + r, :, :] = y[r * width : (r + 1) * width, :]


def project_keys(x_ref, w_ref, out_ref, v_ref, vt_ref):
    rows, width, dim = v_ref.shape
    chunk = 256
    for c in range(0, x_ref.shape[0], chunk):
        y = jnp.dot(x_ref[c : c + chunk, :], w_ref[...], preferred_element_type=F32).astype(BF16)
        for r in range(c // width, (c + chunk) // width):
            vt_ref[:, :, r * width : (r + 1) * width] = v_ref[r].T.reshape(HEADS, dim // HEADS, width)
        for block in range(out_ref.shape[0]):
            out_ref[block, c : c + chunk, :] = y[:, block * LANES : (block + 1) * LANES]


def token_bias(tissue_ref, bias_ref):
    rows, width = tissue_ref.shape
    for r in range(rows):
        bias = jnp.where(tissue_ref[r : r + 1, :] > 0, 0.0, NONE)
        bias_ref[r * width : (r + 1) * width, :] = jnp.broadcast_to(bias, (LANES, width)).T


def score_chunk(pair, side, c, chunk, bias_ref, heads_ref, k_ref, score_ref, slot, top):
    agents = heads_ref.shape[1]
    s = lax.dot_general(
        k_ref[pair, c : c + chunk, :], heads_ref[2 * pair + side], NT, preferred_element_type=F32
    )
    bias = bias_ref[c : c + chunk, :]
    s = s + jnp.concatenate([bias] * (agents // LANES), axis=1)
    score_ref[slot, side, c : c + chunk, :] = s
    return jnp.maximum(top, jnp.max(s.reshape(chunk // 8, 8, agents), axis=0))


def weigh_chunk(head, side, c, chunk, vt_ref, score_ref, slot, top, total, got):
    agents = score_ref.shape[3]
    e = jnp.exp(score_ref[slot, side, c : c + chunk, :] - top)
    total = total + jnp.sum(e.reshape(chunk // 8, 8, agents), axis=0)
    part = jnp.dot(vt_ref[head, :, c : c + chunk], e.astype(BF16), preferred_element_type=F32)
    return total, part if got is None else got + part


def band_stats(after, before, bias_ref, heads_ref, k_ref, vt_ref, score_ref, w_ref, mt_ref, slot, tops):
    tokens = k_ref.shape[1]
    agents = heads_ref.shape[1]
    chunk = 256
    found = []
    for side in range(2):
        top = jnp.full((8, agents), NONE, F32)
        total, got = jnp.zeros((8, agents), F32), None
        if before is not None:
            head = 2 * before + side
            peak = jnp.maximum(tops[side], 0.1 * NONE)
        for c in range(0, tokens, chunk):
            if after is not None:
                top = score_chunk(after, side, c, chunk, bias_ref, heads_ref, k_ref, score_ref, slot, top)
            if before is not None:
                total, got = weigh_chunk(head, side, c, chunk, vt_ref, score_ref, 1 - slot, peak, total, got)
        found.append(jnp.max(top, axis=0, keepdims=True))
        if before is not None:
            w_ref[head, :, :] = got
            mt_ref[head, 0:1, :] = tops[side]
            mt_ref[head, 1:2, :] = jnp.sum(total, axis=0, keepdims=True)
    return found


def token_side(x_ref, wq_ref, heads_ref, tw_ref):
    tokens = x_ref.shape[0]
    chunk, part = 256, 128

    for c in range(0, tokens, chunk):
        q = jnp.dot(x_ref[c : c + chunk, :], wq_ref[...], preferred_element_type=F32).astype(BF16)
        for head in range(HEADS):
            start = head // 2 * LANES
            for p in range(0, chunk, part):
                s = lax.dot_general(
                    heads_ref[head], q[p : p + part, start : start + LANES], NT, preferred_element_type=F32
                )
                e = jnp.exp(s - jnp.max(s, axis=0, keepdims=True))
                share = 1.0 / jnp.sum(e, axis=0, keepdims=True)
                tw_ref[head, :, c + p : c + p + part] = (e * share).astype(BF16)


POINTS = (1.0, -1.0, 2.0, -2.0, 0.5, -0.5)
NORMS = (-4.5, 4.5, 45.0, -45.0, 2.8125, -2.8125)
PLANES = 13


def spread_taps(k7_ref, k5_ref, k3_ref, sum_ref, taps_ref):
    for p in range(7):
        sum_ref[p, 0:7, :] = k7_ref[p]
    for p in range(5):
        sum_ref[p + 1, 1:6, :] = sum_ref[p + 1, 1:6, :] + k5_ref[p]
    for p in range(3):
        sum_ref[p + 2, 2:5, :] = sum_ref[p + 2, 2:5, :] + k3_ref[p]

    def one(block, carry):
        at = pl.ds(pl.multiple_of(block * LANES, LANES), LANES)
        g = [sum_ref[p, 0:7, at] for p in range(7)]
        planes = []
        for first, count in ((0, 4), (4, 3)):
            for point, norm in zip(POINTS, NORMS):
                total = g[first] * (1.0 / norm)
                for j in range(1, count):
                    total = total + g[first + j] * (point**j / norm)
                planes.append(total)
        planes.append(g[3])
        for i, plane in enumerate(planes):
            for q in range(7):
                taps_ref[block, i * 7 + q, :, :] = jnp.broadcast_to(plane[q : q + 1], (8, LANES))
        return carry

    lax.fori_loop(0, taps_ref.shape[0], one, 0)


def fill_sides(ext_ref):
    blocks, planes, padded, _ = ext_ref.shape
    for block in range(blocks):
        for r in range(planes):
            ext_ref[block, r, 0:8, :] = jnp.zeros((8, LANES), F32)
            ext_ref[block, r, padded - 8 : padded, :] = jnp.zeros((8, LANES), F32)


def at_points(d, last):
    planes = []
    e, o = d[0] + d[4] - 4.25 * d[2], d[1] + d[5] - 4.25 * d[3]
    planes += [o + e, o - e]
    e, o = 0.5 * d[0] - 2.5 * d[2] + 2.0 * d[4], 0.25 * d[1] - 1.25 * d[3] + d[5]
    planes += [o + e, o - e]
    e, o = 2.0 * d[0] - 2.5 * d[2] + 0.5 * d[4], 4.0 * d[1] - 5.0 * d[3] + d[5]
    planes += [o + e, o - e]
    if last:
        planes.append(d[6] - d[0] + 5.25 * (d[2] - d[4]))
    return planes


def transform_own(v_ref, ext_ref):
    rows, width, _ = v_ref.shape
    step = 16

    def one(block, carry):
        at = pl.ds(pl.multiple_of(block * LANES, LANES), LANES)
        for c in range(0, width, step):
            where = slice(c, c + step)
            d = [v_ref[r, where, at].astype(F32) for r in range(1, rows)]
            for i, plane in enumerate(at_points(d, True)):
                ext_ref[block, 7 + i, c + 8 : c + 8 + step, :] = plane
        return carry

    lax.fori_loop(0, ext_ref.shape[0], one, 0)


def transform_rims(v_ref, above_ref, below_ref, ext_ref):
    rows, width, _ = v_ref.shape
    step = 16

    def one(block, carry):
        at = pl.ds(pl.multiple_of(block * LANES, LANES), LANES)
        for c in range(0, width, step):
            where = slice(c, c + step)
            d = [above_ref[r, where, at].astype(F32) for r in range(3)]
            d += [v_ref[r, where, at].astype(F32) for r in range(4)]
            for i, plane in enumerate(at_points(d, True)):
                ext_ref[block, i, c + 8 : c + 8 + step, :] = plane
            d = [v_ref[r, where, at].astype(F32) for r in range(rows - 3, rows)]
            d += [below_ref[r, where, at].astype(F32) for r in range(3)]
            for i, plane in enumerate(at_points(d, False)):
                ext_ref[block, 14 + i, c + 8 : c + 8 + step, :] = plane
        return carry

    lax.fori_loop(0, ext_ref.shape[0], one, 0)


def wide_tap(taps_ref, block, plane, q, step):
    return jnp.concatenate([taps_ref[block, plane * 7 + q]] * (step // 8), axis=0)


def convolve_own(ext_ref, taps_ref, part_ref):
    blocks, _, width, _ = part_ref.shape
    step = 16

    def one(block, carry):
        for c in range(0, width, step):
            sums = [None] * PLANES
            for q in range(7):
                for point in range(7):
                    x = ext_ref[block, 7 + point, c + 5 + q : c + 5 + q + step, :]
                    for tile, plane in ((0, 6 + point), (1, point if point < 6 else 12)):
                        if tile == 0 and point == 6:
                            continue
                        term = x * wide_tap(taps_ref, block, plane, q, step)
                        at = 6 * tile + point
                        sums[at] = term if sums[at] is None else sums[at] + term
            for i, total in enumerate(sums):
                part_ref[block, i, c : c + step, :] = total
        return carry

    lax.fori_loop(0, blocks, one, 0)


def convolve(ext_ref, taps_ref, part_ref, pos_ref, first, last):
    width = pos_ref.shape[2]
    step = 16

    def one(block, carry):
        for c in range(0, width, step):
            here = slice(c, c + step)
            m = [
                [part_ref[block, i, here, :] for i in range(6)] + [None],
                [part_ref[block, 6 + i, here, :] for i in range(7)],
            ]
            for q in range(7):
                where = slice(c + 5 + q, c + 5 + q + step)
                for point in range(7):
                    tap = wide_tap(taps_ref, block, point if point < 6 else 12, q, step)
                    term = ext_ref[block, point, where, :] * tap
                    m[0][point] = term if m[0][point] is None else m[0][point] + term
                for point in range(6):
                    tap = wide_tap(taps_ref, block, 6 + point, q, step)
                    m[1][point] = m[1][point] + ext_ref[block, 14 + point, where, :] * tap
            for tile in range(2):
                a = m[tile]
                s1, d1 = a[0] + a[1], a[0] - a[1]
                s2, d2 = a[2] + a[3], a[2] - a[3]
                s3, d3 = a[4] + a[5], a[4] - a[5]
                outs = (
                    s1 + s2 + s3,
                    d1 + 2.0 * d2 + 0.5 * d3,
                    s1 + 4.0 * s2 + 0.25 * s3,
                    d1 + 8.0 * d2 + 0.125 * d3 + a[6],
                )
                for i, y in enumerate(outs):
                    pos_ref[block, tile * 4 + i, here, :] = y
        return carry

    lax.fori_loop(first, last, one, 0)


def blend(first, av_ref, tw_ref, pos_ref, out_ref):
    blocks, _, width, _ = pos_ref.shape
    pieces, piece, _ = av_ref.shape
    per = LANES // piece
    chunk = 256
    for i in range(blocks // 2):
        block = first + i
        av_t = jnp.concatenate([av_ref[block * per + p] for p in range(per)], axis=0)
        lanes = pl.ds(pl.multiple_of(block * LANES, LANES), LANES)
        for c in range(0, out_ref.shape[0], chunk):
            parts = [
                jnp.dot(
                    av_t[side * 64 : side * 64 + 64, :],
                    tw_ref[2 * block + side, :, c : c + chunk],
                    preferred_element_type=F32,
                )
                for side in range(2)
            ]
            attended = jnp.concatenate(parts, axis=0).T
            position = jnp.concatenate(
                [pos_ref[block, r] for r in range(c // width, (c + chunk) // width)], axis=0
            )
            out_ref[c : c + chunk, lanes] = (attended + position).astype(BF16)


class Exchange:
    def __init__(self, n, v_ref, refs, sems):
        self.n, self.me = n, lax.axis_index("col")
        (self.w, self.mt, self.wp, self.mtp, self.ws, self.ms, self.wr, self.mr, self.av,
         above_ref, below_ref) = refs
        s1, r1, s2, r2, s3, r3, s4, r4 = sems
        me, m = self.me, n // 2
        self.m = m
        self.low, self.group = lax.rem(me, 2), me // 2
        twin = me + 1 - 2 * self.low
        self.to = [lax.rem(me + k, n) for k in range(1, n)]
        rows = v_ref.shape[0]
        half = HEADS // 2
        self.mine, self.other = half * self.low, half * (1 - self.low)

        def remote(src, dst, s, r, peer):
            return pltpu.make_async_remote_copy(
                src_ref=src, dst_ref=dst, send_sem=s, recv_sem=r,
                device_id={"col": peer}, device_id_type=pl.DeviceIdType.MESH,
            )

        self.swap = [
            remote(self.w.at[pl.ds(self.other, half)], self.wp, s1.at[0], r1.at[0], twin),
            remote(self.mt.at[pl.ds(self.other, half)], self.mtp, s1.at[1], r1.at[1], twin),
        ]
        self.scatter = []
        self.crossing = []
        for k in range(1, m):
            g = lax.rem(self.group + k, m)
            peer = 2 * g + self.low
            group = self.crossing if k % 2 else self.scatter
            group.append(remote(self.ws.at[g], self.wr.at[self.group], s2.at[0, k - 1], r2.at[0, k - 1], peer))
            group.append(remote(self.ms.at[g], self.mr.at[self.group], s2.at[1, k - 1], r2.at[1, k - 1], peer))
        self.slot = m * self.low + self.group
        self.gather = []
        for k in range(1, m):
            peer = 2 * lax.rem(self.group + k, m) + self.low
            self.gather.append(
                remote(self.av.at[self.slot], self.av.at[self.slot], s4.at[k - 1], r4.at[k - 1], peer)
            )
        own = self.av.at[pl.ds(m * self.low, m)]
        self.forward = remote(own, own, s4.at[m - 1], r4.at[m - 1], twin)
        self.down = remote(v_ref.at[pl.ds(rows - 3, 3)], above_ref, s3.at[0], r3.at[0], lax.rem(me + 1, n))
        self.up = remote(v_ref.at[pl.ds(0, 3)], below_ref, s3.at[1], r3.at[1], lax.rem(me + n - 1, n))

    def greet(self):
        barrier = pltpu.get_barrier_semaphore()
        for p in self.to:
            pl.semaphore_signal(
                barrier, inc=1, device_id={"col": p}, device_id_type=pl.DeviceIdType.MESH
            )

    def met(self):
        pl.semaphore_wait(pltpu.get_barrier_semaphore(), self.n - 1)

    def send_rims(self):
        @pl.when(self.me < self.n - 1)
        def _():
            self.down.start()

        @pl.when(self.me > 0)
        def _():
            self.up.start()

    def send_twin(self):
        for copy in self.swap:
            copy.start()

    def merge(self):
        for copy in self.swap:
            copy.wait()
        half, depth, _ = self.wp.shape
        piece = self.ws.shape[1]
        for h in range(half):
            a, b = self.mt[self.mine + h], self.mtp[h]
            top = jnp.maximum(a[0:1], b[0:1])
            fa, fb = jnp.exp(a[0:1] - top), jnp.exp(b[0:1] - top)
            total = a[1:2] * fa + b[1:2] * fb
            w = self.w[self.mine + h] * fa + self.wp[h] * fb
            for p in range(depth // piece):
                at = h * depth // piece + p
                self.ws[at] = w[p * piece : (p + 1) * piece]
                self.ms[at, 0:1, :] = top
                self.ms[at, 1:2, :] = total
        for copy in self.scatter + self.crossing:
            copy.start()
        self.wr[self.group] = self.ws[self.group]
        self.mr[self.group] = self.ms[self.group]

    def cross(self):
        for copy in self.crossing:
            copy.start()

    def reduce(self):
        for copy in self.scatter + self.crossing:
            copy.wait()
        tops = [self.mr[i, 0:1, :] for i in range(self.m)]
        top = functools.reduce(jnp.maximum, tops)
        total, weighted = 0.0, 0.0
        for i in range(self.m):
            f = jnp.exp(tops[i] - top)
            total = total + f * self.mr[i, 1:2, :]
            weighted = weighted + f * self.wr[i]
        self.av[self.slot] = (weighted / total).astype(BF16)
        for copy in self.gather:
            copy.start()

    def rims(self):
        @pl.when(self.me < self.n - 1)
        def _():
            self.down.wait_send()
            self.up.wait_recv()

        @pl.when(self.me > 0)
        def _():
            self.down.wait_recv()
            self.up.wait_send()

    def pass_on(self):
        for copy in self.gather:
            copy.wait()
        self.forward.start()

    def end(self):
        self.forward.wait()


def sem_shapes(n):
    dma = pltpu.SemaphoreType.DMA
    m = n // 2
    return [dma((2,)), dma((2,)), dma((2, m - 1)), dma((2, m - 1)), dma((2,)), dma((2,)),
            dma((m,)), dma((m,))]


def whole_kernel(n, *refs):
    sources, out_ref = refs[:9], refs[9]
    held, load_sem = refs[10:19], refs[19]
    x_ref, tissue_ref, wq_ref, wk_ref, wv_ref, ag_ref, k7_ref, k5_ref, k3_ref = held
    (v_ref, vt_ref, k_ref, bias_ref, score_ref, tw_ref, sum_ref, taps_ref, ext_ref, part_ref, pos_ref, heads_ref) = refs[20:32]
    shared, sems = refs[32:43], refs[43:]
    w_ref, mt_ref, av_ref, above_ref, below_ref = shared[0], shared[1], shared[8], shared[9], shared[10]
    loads = [pltpu.make_async_copy(sources[i], held[i], load_sem.at[i]) for i in range(9)]
    for i in (5, 1, 0, 4, 3, 2, 6, 7, 8):
        loads[i].start()
    work = Exchange(n, v_ref, shared, sems)

    @pl.when(work.me == 0)
    def _():
        above_ref[...] = jnp.zeros(above_ref.shape, BF16)

    @pl.when(work.me == n - 1)
    def _():
        below_ref[...] = jnp.zeros(below_ref.shape, BF16)

    work.greet()
    loads[5].wait()
    split_agents(ag_ref, heads_ref)
    loads[1].wait()
    token_bias(tissue_ref, bias_ref)
    loads[0].wait()
    loads[4].wait()
    project_values(x_ref, wv_ref, v_ref)
    work.met()
    work.send_rims()
    loads[3].wait()
    project_keys(x_ref, wk_ref, k_ref, v_ref, vt_ref)

    def stats(after, before, slot, tops):
        return band_stats(
            after, before, bias_ref, heads_ref, k_ref, vt_ref, score_ref, w_ref, mt_ref, slot, tops
        )

    order = [work.other // 2 + i for i in range(HEADS // 4)] + [work.mine // 2 + i for i in range(HEADS // 4)]
    tops = None
    for i in range(HEADS // 2 + 1):
        after = order[i] if i < HEADS // 2 else None
        before = order[i - 1] if i > 0 else None
        tops = stats(after, before, i % 2, tops)
        if i == HEADS // 4:
            work.send_twin()
    work.merge()
    for i in (6, 7, 8, 2):
        loads[i].wait()
    fill_sides(ext_ref)
    spread_taps(k7_ref, k5_ref, k3_ref, sum_ref, taps_ref)
    transform_own(v_ref, ext_ref)
    token_side(x_ref, wq_ref, heads_ref, tw_ref)
    convolve_own(ext_ref, taps_ref, part_ref)
    blocks = pos_ref.shape[0]
    work.reduce()
    work.rims()
    transform_rims(v_ref, above_ref, below_ref, ext_ref)
    convolve(ext_ref, taps_ref, part_ref, pos_ref, 0, blocks)
    work.pass_on()
    blend(work.mine // 2, av_ref, tw_ref, pos_ref, out_ref)
    work.end()
    blend(work.other // 2, av_ref, tw_ref, pos_ref, out_ref)


def on_device(n, patches, tissue, w_query, w_key, w_value, w_out, agent_tokens, k7, k5, k3):
    rows, width, dim = patches.shape
    tokens = rows * width
    agents = agent_tokens.shape[0]
    x = patches.reshape(tokens, dim)
    rim = (3, width, dim)
    blocks = dim // LANES
    depth, half, m = dim // HEADS, HEADS // 2, n // 2
    piece = dim // n
    given = (x, tissue, w_query, w_key, w_value, agent_tokens, k7, k5, k3)
    blended = pl.pallas_call(
        functools.partial(whole_kernel, n),
        out_shape=pltpu.VMEM((tokens, dim), BF16),
        in_specs=[pl.BlockSpec(memory_space=pltpu.HBM)] * len(given),
        out_specs=VMEM,
        scratch_shapes=[pltpu.VMEM(a.shape, a.dtype) for a in given]
        + [
            pltpu.SemaphoreType.DMA((len(given),)),
            pltpu.VMEM((rows, width, dim), BF16),
            pltpu.VMEM((HEADS, depth, tokens), BF16),
            pltpu.VMEM((blocks, tokens, LANES), BF16),
            pltpu.VMEM((tokens, LANES), F32),
            pltpu.VMEM((2, 2, tokens, agents), F32),
            pltpu.VMEM((HEADS, agents, tokens), BF16),
            pltpu.VMEM((7, 8, dim), F32),
            pltpu.VMEM((blocks, 7 * PLANES, 8, LANES), F32),
            pltpu.VMEM((blocks, 20, width + 16, LANES), F32),
            pltpu.VMEM((blocks, PLANES, width, LANES), F32),
            pltpu.VMEM((blocks, rows, width, LANES), F32),
            pltpu.VMEM((HEADS, agents, LANES), BF16),
            pltpu.VMEM((HEADS, depth, agents), F32),
            pltpu.VMEM((HEADS, 2, agents), F32),
            pltpu.VMEM((half, depth, agents), F32),
            pltpu.VMEM((half, 2, agents), F32),
            pltpu.VMEM((m, piece, agents), F32),
            pltpu.VMEM((m, 2, agents), F32),
            pltpu.VMEM((m, piece, agents), F32),
            pltpu.VMEM((m, 2, agents), F32),
            pltpu.VMEM((n, piece, agents), BF16),
            pltpu.VMEM(rim, BF16),
            pltpu.VMEM(rim, BF16),
        ]
        + sem_shapes(n),
        compiler_params=pltpu.CompilerParams(
            vmem_limit_bytes=LIMIT, collective_id=0, has_side_effects=True
        ),
    )(*given)
    mixed = jnp.dot(blended, w_out, preferred_element_type=F32).astype(BF16)
    return mixed.reshape(rows, width, dim)


def solution(mesh):
    rows = P(("slide", "col"), None, None)
    return jax.shard_map(
        functools.partial(on_device, mesh.shape["col"]),
        mesh=mesh,
        in_specs=(rows, P(("slide", "col"), None)) + (P(),) * 8,
        out_specs=rows,
        check_vma=False,
    )
```

```python
import functools

import jax
import jax.numpy as jnp
from jax import lax
from jax.experimental import pallas as pl
from jax.experimental.pallas import tpu as pltpu
from jax.sharding import PartitionSpec as P

HEADS = 8
LANES = 128
NONE = -1e30
F32, BF16 = jnp.float32, jnp.bfloat16
NT = (((1,), (1,)), ((), ()))
VMEM = pl.BlockSpec(memory_space=pltpu.VMEM)
LIMIT = 56 * 1024 * 1024


def low_half(shape):
    return lax.broadcasted_iota(jnp.int32, shape, len(shape) - 1) < LANES // 2


def head_agents(ag_ref, head):
    start = head // 2 * LANES
    pair = ag_ref[:, start : start + LANES].astype(F32) * 0.125
    keep = low_half(pair.shape)
    keep = keep if head % 2 == 0 else jnp.logical_not(keep)
    return jnp.where(keep, pair, 0.0).astype(BF16)


def split_agents(ag_ref, heads_ref):
    for head in range(HEADS):
        heads_ref[head, :, :] = head_agents(ag_ref, head)


def project_values(x_ref, w_ref, out_ref):
    rows, width, dim = out_ref.shape
    chunk = 256
    for c in range(0, x_ref.shape[0], chunk):
        y = jnp.dot(x_ref[c : c + chunk, :], w_ref[...], preferred_element_type=F32).astype(BF16)
        for r in range(chunk // width):
            out_ref[c // width + r, :, :] = y[r * width : (r + 1) * width, :]


def project_keys(x_ref, w_ref, out_ref, v_ref, vt_ref):
    rows, width, dim = v_ref.shape
    chunk = 256
    for c in range(0, x_ref.shape[0], chunk):
        y = jnp.dot(x_ref[c : c + chunk, :], w_ref[...], preferred_element_type=F32).astype(BF16)
        for r in range(c // width, (c + chunk) // width):
            vt_ref[:, :, r * width : (r + 1) * width] = v_ref[r].T.reshape(HEADS, dim // HEADS, width)
        for block in range(out_ref.shape[0]):
            out_ref[block, c : c + chunk, :] = y[:, block * LANES : (block + 1) * LANES]


def token_bias(tissue_ref, bias_ref):
    rows, width = tissue_ref.shape
    for r in range(rows):
        bias = jnp.where(tissue_ref[r : r + 1, :] > 0, 0.0, NONE)
        bias_ref[r * width : (r + 1) * width, :] = jnp.broadcast_to(bias, (LANES, width)).T


def score_chunk(pair, side, c, chunk, bias_ref, heads_ref, k_ref, score_ref, slot, top):
    agents = heads_ref.shape[1]
    s = lax.dot_general(
        k_ref[pair, c : c + chunk, :], heads_ref[2 * pair + side], NT, preferred_element_type=F32
    )
    bias = bias_ref[c : c + chunk, :]
    s = s + jnp.concatenate([bias] * (agents // LANES), axis=1)
    score_ref[slot, side, c : c + chunk, :] = s
    return jnp.maximum(top, jnp.max(s.reshape(chunk // 8, 8, agents), axis=0))


def weigh_chunk(head, side, c, chunk, vt_ref, score_ref, slot, top, total, got):
    agents = score_ref.shape[3]
    e = jnp.exp(score_ref[slot, side, c : c + chunk, :] - top)
    total = total + jnp.sum(e.reshape(chunk // 8, 8, agents), axis=0)
    part = jnp.dot(vt_ref[head, :, c : c + chunk], e.astype(BF16), preferred_element_type=F32)
    return total, part if got is None else got + part


def band_stats(after, before, bias_ref, heads_ref, k_ref, vt_ref, score_ref, w_ref, mt_ref, slot, tops):
    tokens = k_ref.shape[1]
    agents = heads_ref.shape[1]
    chunk = 256
    found = []
    for side in range(2):
        top = jnp.full((8, agents), NONE, F32)
        total, got = jnp.zeros((8, agents), F32), None
        if before is not None:
            head = 2 * before + side
            peak = jnp.maximum(tops[side], 0.1 * NONE)
        for c in range(0, tokens, chunk):
            if after is not None:
                top = score_chunk(after, side, c, chunk, bias_ref, heads_ref, k_ref, score_ref, slot, top)
            if before is not None:
                total, got = weigh_chunk(head, side, c, chunk, vt_ref, score_ref, 1 - slot, peak, total, got)
        found.append(jnp.max(top, axis=0, keepdims=True))
        if before is not None:
            w_ref[head, :, :] = got
            mt_ref[head, 0:1, :] = tops[side]
            mt_ref[head, 1:2, :] = jnp.sum(total, axis=0, keepdims=True)
    return found


def token_side(x_ref, wq_ref, heads_ref, tw_ref):
    tokens = x_ref.shape[0]
    chunk, part = 256, 128

    for c in range(0, tokens, chunk):
        q = jnp.dot(x_ref[c : c + chunk, :], wq_ref[...], preferred_element_type=F32).astype(BF16)
        for head in range(HEADS):
            start = head // 2 * LANES
            for p in range(0, chunk, part):
                s = lax.dot_general(
                    heads_ref[head], q[p : p + part, start : start + LANES], NT, preferred_element_type=F32
                )
                e = jnp.exp(s - jnp.max(s, axis=0, keepdims=True))
                share = 1.0 / jnp.sum(e, axis=0, keepdims=True)
                tw_ref[head, :, c + p : c + p + part] = (e * share).astype(BF16)


POINTS = (1.0, -1.0, 2.0, -2.0, 0.5, -0.5)
NORMS = (-4.5, 4.5, 45.0, -45.0, 2.8125, -2.8125)
PLANES = 13


def spread_taps(k7_ref, k5_ref, k3_ref, sum_ref, taps_ref):
    for p in range(7):
        sum_ref[p, 0:7, :] = k7_ref[p]
    for p in range(5):
        sum_ref[p + 1, 1:6, :] = sum_ref[p + 1, 1:6, :] + k5_ref[p]
    for p in range(3):
        sum_ref[p + 2, 2:5, :] = sum_ref[p + 2, 2:5, :] + k3_ref[p]

    def one(block, carry):
        at = pl.ds(pl.multiple_of(block * LANES, LANES), LANES)
        g = [sum_ref[p, 0:7, at] for p in range(7)]
        planes = []
        for first, count in ((0, 4), (4, 3)):
            for point, norm in zip(POINTS, NORMS):
                total = g[first] * (1.0 / norm)
                for j in range(1, count):
                    total = total + g[first + j] * (point**j / norm)
                planes.append(total)
        planes.append(g[3])
        for i, plane in enumerate(planes):
            for q in range(7):
                taps_ref[block, i * 7 + q, :, :] = jnp.broadcast_to(plane[q : q + 1], (8, LANES))
        return carry

    lax.fori_loop(0, taps_ref.shape[0], one, 0)


def fill_sides(ext_ref):
    blocks, planes, padded, _ = ext_ref.shape
    for block in range(blocks):
        for r in range(planes):
            ext_ref[block, r, 0:8, :] = jnp.zeros((8, LANES), F32)
            ext_ref[block, r, padded - 8 : padded, :] = jnp.zeros((8, LANES), F32)


def at_points(d, last):
    planes = []
    e, o = d[0] + d[4] - 4.25 * d[2], d[1] + d[5] - 4.25 * d[3]
    planes += [o + e, o - e]
    e, o = 0.5 * d[0] - 2.5 * d[2] + 2.0 * d[4], 0.25 * d[1] - 1.25 * d[3] + d[5]
    planes += [o + e, o - e]
    e, o = 2.0 * d[0] - 2.5 * d[2] + 0.5 * d[4], 4.0 * d[1] - 5.0 * d[3] + d[5]
    planes += [o + e, o - e]
    if last:
        planes.append(d[6] - d[0] + 5.25 * (d[2] - d[4]))
    return planes


def transform_own(v_ref, ext_ref):
    rows, width, _ = v_ref.shape
    step = 16

    def one(block, carry):
        at = pl.ds(pl.multiple_of(block * LANES, LANES), LANES)
        for c in range(0, width, step):
            where = slice(c, c + step)
            d = [v_ref[r, where, at].astype(F32) for r in range(1, rows)]
            for i, plane in enumerate(at_points(d, True)):
                ext_ref[block, 7 + i, c + 8 : c + 8 + step, :] = plane
        return carry

    lax.fori_loop(0, ext_ref.shape[0], one, 0)


def transform_rims(v_ref, above_ref, below_ref, ext_ref):
    rows, width, _ = v_ref.shape
    step = 16

    def one(block, carry):
        at = pl.ds(pl.multiple_of(block * LANES, LANES), LANES)
        for c in range(0, width, step):
            where = slice(c, c + step)
            d = [above_ref[r, where, at].astype(F32) for r in range(3)]
            d += [v_ref[r, where, at].astype(F32) for r in range(4)]
            for i, plane in enumerate(at_points(d, True)):
                ext_ref[block, i, c + 8 : c + 8 + step, :] = plane
            d = [v_ref[r, where, at].astype(F32) for r in range(rows - 3, rows)]
            d += [below_ref[r, where, at].astype(F32) for r in range(3)]
            for i, plane in enumerate(at_points(d, False)):
                ext_ref[block, 14 + i, c + 8 : c + 8 + step, :] = plane
        return carry

    lax.fori_loop(0, ext_ref.shape[0], one, 0)


def wide_tap(taps_ref, block, plane, q, step):
    return jnp.concatenate([taps_ref[block, plane * 7 + q]] * (step // 8), axis=0)


def convolve_own(ext_ref, taps_ref, part_ref):
    blocks, _, width, _ = part_ref.shape
    step = 16

    def one(block, carry):
        for c in range(0, width, step):
            sums = [None] * PLANES
            for q in range(7):
                for point in range(7):
                    x = ext_ref[block, 7 + point, c + 5 + q : c + 5 + q + step, :]
                    for tile, plane in ((0, 6 + point), (1, point if point < 6 else 12)):
                        if tile == 0 and point == 6:
                            continue
                        term = x * wide_tap(taps_ref, block, plane, q, step)
                        at = 6 * tile + point
                        sums[at] = term if sums[at] is None else sums[at] + term
            for i, total in enumerate(sums):
                part_ref[block, i, c : c + step, :] = total
        return carry

    lax.fori_loop(0, blocks, one, 0)


def convolve(ext_ref, taps_ref, part_ref, pos_ref, first, last):
    width = pos_ref.shape[2]
    step = 16

    def one(block, carry):
        for c in range(0, width, step):
            here = slice(c, c + step)
            m = [
                [part_ref[block, i, here, :] for i in range(6)] + [None],
                [part_ref[block, 6 + i, here, :] for i in range(7)],
            ]
            for q in range(7):
                where = slice(c + 5 + q, c + 5 + q + step)
                for point in range(7):
                    tap = wide_tap(taps_ref, block, point if point < 6 else 12, q, step)
                    term = ext_ref[block, point, where, :] * tap
                    m[0][point] = term if m[0][point] is None else m[0][point] + term
                for point in range(6):
                    tap = wide_tap(taps_ref, block, 6 + point, q, step)
                    m[1][point] = m[1][point] + ext_ref[block, 14 + point, where, :] * tap
            for tile in range(2):
                a = m[tile]
                s1, d1 = a[0] + a[1], a[0] - a[1]
                s2, d2 = a[2] + a[3], a[2] - a[3]
                s3, d3 = a[4] + a[5], a[4] - a[5]
                outs = (
                    s1 + s2 + s3,
                    d1 + 2.0 * d2 + 0.5 * d3,
                    s1 + 4.0 * s2 + 0.25 * s3,
                    d1 + 8.0 * d2 + 0.125 * d3 + a[6],
                )
                for i, y in enumerate(outs):
                    pos_ref[block, tile * 4 + i, here, :] = y
        return carry

    lax.fori_loop(first, last, one, 0)


def blend(first, av_ref, tw_ref, pos_ref, out_ref):
    blocks, _, width, _ = pos_ref.shape
    pieces, piece, _ = av_ref.shape
    per = LANES // piece
    chunk = 256
    for i in range(blocks // 2):
        block = first + i
        av_t = jnp.concatenate([av_ref[block * per + p] for p in range(per)], axis=0)
        lanes = pl.ds(pl.multiple_of(block * LANES, LANES), LANES)
        for c in range(0, out_ref.shape[0], chunk):
            parts = [
                jnp.dot(
                    av_t[side * 64 : side * 64 + 64, :],
                    tw_ref[2 * block + side, :, c : c + chunk],
                    preferred_element_type=F32,
                )
                for side in range(2)
            ]
            attended = jnp.concatenate(parts, axis=0).T
            position = jnp.concatenate(
                [pos_ref[block, r] for r in range(c // width, (c + chunk) // width)], axis=0
            )
            out_ref[c : c + chunk, lanes] = (attended + position).astype(BF16)


class Exchange:
    def __init__(self, n, v_ref, refs, sems):
        self.n, self.me = n, lax.axis_index("col")
        (self.w, self.mt, self.wp, self.mtp, self.ws, self.ms, self.wr, self.mr, self.av,
         above_ref, below_ref) = refs
        s1, r1, s2, r2, s3, r3, s4, r4 = sems
        me, m = self.me, n // 2
        self.m = m
        self.low, self.group = lax.rem(me, 2), me // 2
        twin = me + 1 - 2 * self.low
        self.to = [lax.rem(me + k, n) for k in range(1, n)]
        rows = v_ref.shape[0]
        half = HEADS // 2
        self.mine, self.other = half * self.low, half * (1 - self.low)

        def remote(src, dst, s, r, peer):
            return pltpu.make_async_remote_copy(
                src_ref=src, dst_ref=dst, send_sem=s, recv_sem=r,
                device_id={"col": peer}, device_id_type=pl.DeviceIdType.MESH,
            )

        self.swap = [
            remote(self.w.at[pl.ds(self.other, half)], self.wp, s1.at[0], r1.at[0], twin),
            remote(self.mt.at[pl.ds(self.other, half)], self.mtp, s1.at[1], r1.at[1], twin),
        ]
        self.scatter = []
        self.crossing = []
        for k in range(1, m):
            g = lax.rem(self.group + k, m)
            peer = 2 * g + self.low
            group = self.scatter
            group.append(remote(self.ws.at[g], self.wr.at[self.group], s2.at[0, k - 1], r2.at[0, k - 1], peer))
            group.append(remote(self.ms.at[g], self.mr.at[self.group], s2.at[1, k - 1], r2.at[1, k - 1], peer))
        self.slot = m * self.low + self.group
        self.gather = []
        for k in range(1, m):
            peer = 2 * lax.rem(self.group + k, m) + self.low
            self.gather.append(
                remote(self.av.at[self.slot], self.av.at[self.slot], s4.at[k - 1], r4.at[k - 1], peer)
            )
        own = self.av.at[pl.ds(m * self.low, m)]
        self.forward = remote(own, own, s4.at[m - 1], r4.at[m - 1], twin)
        self.down = remote(v_ref.at[pl.ds(rows - 3, 3)], above_ref, s3.at[0], r3.at[0], lax.rem(me + 1, n))
        self.up = remote(v_ref.at[pl.ds(0, 3)], below_ref, s3.at[1], r3.at[1], lax.rem(me + n - 1, n))

    def greet(self):
        barrier = pltpu.get_barrier_semaphore()
        for p in self.to:
            pl.semaphore_signal(
                barrier, inc=1, device_id={"col": p}, device_id_type=pl.DeviceIdType.MESH
            )

    def met(self):
        pl.semaphore_wait(pltpu.get_barrier_semaphore(), self.n - 1)

    def send_rims(self):
        @pl.when(self.me < self.n - 1)
        def _():
            self.down.start()

        @pl.when(self.me > 0)
        def _():
            self.up.start()

    def send_twin(self):
        for copy in self.swap:
            copy.start()

    def merge(self):
        for copy in self.swap:
            copy.wait()
        half, depth, _ = self.wp.shape
        piece = self.ws.shape[1]
        for h in range(half):
            a, b = self.mt[self.mine + h], self.mtp[h]
            top = jnp.maximum(a[0:1], b[0:1])
            fa, fb = jnp.exp(a[0:1] - top), jnp.exp(b[0:1] - top)
            total = a[1:2] * fa + b[1:2] * fb
            w = self.w[self.mine + h] * fa + self.wp[h] * fb
            for p in range(depth // piece):
                at = h * depth // piece + p
                self.ws[at] = w[p * piece : (p + 1) * piece]
                self.ms[at, 0:1, :] = top
                self.ms[at, 1:2, :] = total
        for copy in self.scatter + self.crossing:
            copy.start()
        self.wr[self.group] = self.ws[self.group]
        self.mr[self.group] = self.ms[self.group]

    def cross(self):
        for copy in self.crossing:
            copy.start()

    def reduce(self):
        for copy in self.scatter + self.crossing:
            copy.wait()
        tops = [self.mr[i, 0:1, :] for i in range(self.m)]
        top = functools.reduce(jnp.maximum, tops)
        total, weighted = 0.0, 0.0
        for i in range(self.m):
            f = jnp.exp(tops[i] - top)
            total = total + f * self.mr[i, 1:2, :]
            weighted = weighted + f * self.wr[i]
        self.av[self.slot] = (weighted / total).astype(BF16)
        for copy in self.gather:
            copy.start()

    def rims(self):
        @pl.when(self.me < self.n - 1)
        def _():
            self.down.wait_send()
            self.up.wait_recv()

        @pl.when(self.me > 0)
        def _():
            self.down.wait_recv()
            self.up.wait_send()

    def pass_on(self):
        for copy in self.gather:
            copy.wait()
        self.forward.start()

    def end(self):
        self.forward.wait()


def sem_shapes(n):
    dma = pltpu.SemaphoreType.DMA
    m = n // 2
    return [dma((2,)), dma((2,)), dma((2, m - 1)), dma((2, m - 1)), dma((2,)), dma((2,)),
            dma((m,)), dma((m,))]


def whole_kernel(n, *refs):
    sources, out_ref = refs[:9], refs[9]
    held, load_sem = refs[10:19], refs[19]
    x_ref, tissue_ref, wq_ref, wk_ref, wv_ref, ag_ref, k7_ref, k5_ref, k3_ref = held
    (v_ref, vt_ref, k_ref, bias_ref, score_ref, tw_ref, sum_ref, taps_ref, ext_ref, part_ref, pos_ref, heads_ref) = refs[20:32]
    shared, sems = refs[32:43], refs[43:]
    w_ref, mt_ref, av_ref, above_ref, below_ref = shared[0], shared[1], shared[8], shared[9], shared[10]
    loads = [pltpu.make_async_copy(sources[i], held[i], load_sem.at[i]) for i in range(9)]
    for i in (5, 1, 0, 4, 3, 2, 6, 7, 8):
        loads[i].start()
    work = Exchange(n, v_ref, shared, sems)

    @pl.when(work.me == 0)
    def _():
        above_ref[...] = jnp.zeros(above_ref.shape, BF16)

    @pl.when(work.me == n - 1)
    def _():
        below_ref[...] = jnp.zeros(below_ref.shape, BF16)

    work.greet()
    loads[5].wait()
    split_agents(ag_ref, heads_ref)
    loads[1].wait()
    token_bias(tissue_ref, bias_ref)
    loads[0].wait()
    loads[4].wait()
    project_values(x_ref, wv_ref, v_ref)
    work.met()
    work.send_rims()
    loads[3].wait()
    project_keys(x_ref, wk_ref, k_ref, v_ref, vt_ref)

    def stats(after, before, slot, tops):
        return band_stats(
            after, before, bias_ref, heads_ref, k_ref, vt_ref, score_ref, w_ref, mt_ref, slot, tops
        )

    order = [work.other // 2 + i for i in range(HEADS // 4)] + [work.mine // 2 + i for i in range(HEADS // 4)]
    tops = None
    for i in range(HEADS // 2 + 1):
        after = order[i] if i < HEADS // 2 else None
        before = order[i - 1] if i > 0 else None
        tops = stats(after, before, i % 2, tops)
        if i == HEADS // 4:
            work.send_twin()
    work.merge()
    for i in (6, 7, 8, 2):
        loads[i].wait()
    fill_sides(ext_ref)
    spread_taps(k7_ref, k5_ref, k3_ref, sum_ref, taps_ref)
    transform_own(v_ref, ext_ref)
    token_side(x_ref, wq_ref, heads_ref, tw_ref)
    convolve_own(ext_ref, taps_ref, part_ref)
    blocks = pos_ref.shape[0]
    work.reduce()
    work.rims()
    transform_rims(v_ref, above_ref, below_ref, ext_ref)
    convolve(ext_ref, taps_ref, part_ref, pos_ref, 0, blocks)
    work.pass_on()
    blend(work.mine // 2, av_ref, tw_ref, pos_ref, out_ref)
    work.end()
    blend(work.other // 2, av_ref, tw_ref, pos_ref, out_ref)


def on_device(n, patches, tissue, w_query, w_key, w_value, w_out, agent_tokens, k7, k5, k3):
    rows, width, dim = patches.shape
    tokens = rows * width
    agents = agent_tokens.shape[0]
    x = patches.reshape(tokens, dim)
    rim = (3, width, dim)
    blocks = dim // LANES
    depth, half, m = dim // HEADS, HEADS // 2, n // 2
    piece = dim // n
    given = (x, tissue, w_query, w_key, w_value, agent_tokens, k7, k5, k3)
    blended = pl.pallas_call(
        functools.partial(whole_kernel, n),
        out_shape=pltpu.VMEM((tokens, dim), BF16),
        in_specs=[pl.BlockSpec(memory_space=pltpu.HBM)] * len(given),
        out_specs=VMEM,
        scratch_shapes=[pltpu.VMEM(a.shape, a.dtype) for a in given]
        + [
            pltpu.SemaphoreType.DMA((len(given),)),
            pltpu.VMEM((rows, width, dim), BF16),
            pltpu.VMEM((HEADS, depth, tokens), BF16),
            pltpu.VMEM((blocks, tokens, LANES), BF16),
            pltpu.VMEM((tokens, LANES), F32),
            pltpu.VMEM((2, 2, tokens, agents), F32),
            pltpu.VMEM((HEADS, agents, tokens), BF16),
            pltpu.VMEM((7, 8, dim), F32),
            pltpu.VMEM((blocks, 7 * PLANES, 8, LANES), F32),
            pltpu.VMEM((blocks, 20, width + 16, LANES), F32),
            pltpu.VMEM((blocks, PLANES, width, LANES), F32),
            pltpu.VMEM((blocks, rows, width, LANES), F32),
            pltpu.VMEM((HEADS, agents, LANES), BF16),
            pltpu.VMEM((HEADS, depth, agents), F32),
            pltpu.VMEM((HEADS, 2, agents), F32),
            pltpu.VMEM((half, depth, agents), F32),
            pltpu.VMEM((half, 2, agents), F32),
            pltpu.VMEM((m, piece, agents), F32),
            pltpu.VMEM((m, 2, agents), F32),
            pltpu.VMEM((m, piece, agents), F32),
            pltpu.VMEM((m, 2, agents), F32),
            pltpu.VMEM((n, piece, agents), BF16),
            pltpu.VMEM(rim, BF16),
            pltpu.VMEM(rim, BF16),
        ]
        + sem_shapes(n),
        compiler_params=pltpu.CompilerParams(
            vmem_limit_bytes=LIMIT, collective_id=0, has_side_effects=True
        ),
    )(*given)
    mixed = jnp.dot(blended, w_out, preferred_element_type=F32).astype(BF16)
    return mixed.reshape(rows, width, dim)


def solution(mesh):
    rows = P(("slide", "col"), None, None)
    return jax.shard_map(
        functools.partial(on_device, mesh.shape["col"]),
        mesh=mesh,
        in_specs=(rows, P(("slide", "col"), None)) + (P(),) * 8,
        out_specs=rows,
        check_vma=False,
    )
```
